32 devices in a mesh: ctx: 4 (over y, core), fsdp: 8 (over z, x).
Axes of the slice: x: 2, y: 2, z: 4, core: 2. Of those that a mesh axis runs over, the one named last changes fastest.
Arguments:
- tokens: bfloat16 [8, 1024, 512], P('fsdp', 'ctx'), may hold values from -6 to 6
- segment_ids: int32 [8, 1024], P('fsdp'), may hold values from 0 to 3, never falling along the last dimension, each value on 1 to 384 neighbouring positions
- bucket_table: int32 [1024], replicated, may hold values from 0 to 31
- w_qkv: bfloat16 [512, 1536], P('fsdp'), may hold values from -0.25 to 0.25
- w_out: bfloat16 [512, 512], P('fsdp'), may hold values from -2 to 2
- w_in: bfloat16 [512, 2048], P('fsdp'), may hold values from -0.25 to 0.25
- w_down: bfloat16 [2048, 512], P('fsdp'), may hold values from -0.125 to 0.125
- gain_one: bfloat16 [512], P('fsdp'), may hold values from 0.5 to 1.5
- shift_one: bfloat16 [512], P('fsdp'), may hold values from -1.75 to 1.75
- gain_two: bfloat16 [512], P('fsdp'), may hold values from 0.5 to 1.5
- shift_two: bfloat16 [512], P('fsdp'), may hold values from -1.75 to 1.75
- bias_in: bfloat16 [2048], P('fsdp'), may hold values from -1.75 to 1.75
- bias_down: bfloat16 [512], P('fsdp'), may hold values from -1.75 to 1.75
- rel_bias: bfloat16 [32, 8], replicated, may hold values from -6 to 6
- cotangent: bfloat16 [8, 1024, 512], P('fsdp', 'ctx'), may hold values from -6 to 6
Outputs:
- output: bfloat16 [8, 1024, 512], P('fsdp', 'ctx')
- input_grad: bfloat16 [8, 1024, 512], P('fsdp', 'ctx')
- grad_qkv: float32 [512, 1536], P('fsdp')
- grad_out: float32 [512, 512], P('fsdp')
- grad_in: float32 [512, 2048], P('fsdp')
- grad_down: float32 [2048, 512], P('fsdp')
- grad_gain_one: float32 [512], P('fsdp')
- grad_shift_one: float32 [512], P('fsdp')
- grad_gain_two: float32 [512], P('fsdp')
- grad_shift_two: float32 [512], P('fsdp')
- grad_bias_in: float32 [2048], P('fsdp')
- grad_bias_down: float32 [512], P('fsdp')
- grad_rel_bias: float32 [32, 8], replicated
The draws below stay inside these ranges and needn't reach their ends.
Inputs may be any that keep to these rules, and one draw needn't show every extreme that they name: `segment_ids`: along each group the segment number never falls; segment 0 is the group's prompt and segment k > 0 its k-th continuation; each segment has 1 to 384 tokens, one exactly 384.
All inputs are finite; a program needn't handle non-finite values.
Results may differ from the reference program's by a relative error of at most 0.024.
Values may be sent and summed in bfloat16 or wider, within the bound.
A program may use at most 128 MiB of HBM per device.

```python
import math
import jax
import jax.numpy as jnp
import numpy as np
from jax import lax

D = 512
HEADS = 8
HEAD = 64
FF = 2048
NBUCKET = 32
NCONT = 3
GROUP = 1024
GROUPS = 8
SEG_MOST = 384


def touch_ends(array, stream_key, low, high):
    dims = array.shape
    place = [jax.random.randint(jax.random.fold_in(stream_key, axis), (), 0, dims[axis]) for axis in range(len(dims))]
    array = array.at[tuple(place)].set(low)
    longest = dims.index(max(dims))
    place[longest] = (place[longest] + 1) % dims[longest]
    return array.at[tuple(place)].set(high)


def steps_of(rng, extent, cuts, smallest, largest):
    level, own = 1.0, jax.random.fold_in(rng, 6)
    for axis_at, shards_of in cuts:
        heights = jnp.exp(jax.random.uniform(jax.random.fold_in(own, axis_at), (shards_of,), jnp.float32, smallest / len(cuts), largest / len(cuts)))
        level = level * jnp.repeat(heights, extent[axis_at] // shards_of).reshape([-1 if axis == axis_at else 1 for axis in range(len(extent))])
    return level


def length_profile(amount, total, reach, slope):
    portions = [(1 << 20) // math.isqrt(rank ** slope) + 1 for rank in range(2, amount + 1)]
    spare, counts = total - reach - (amount - 1), [1] * (amount - 1)
    while spare > 0:
        movable = [i for i in range(amount - 1) if counts[i] < reach]
        pool, budget = sum([portions[i] for i in movable]), spare
        for i in movable:
            addition = min(reach - counts[i], max(1, budget * portions[i] // pool), spare)
            counts[i] = counts[i] + addition
            spare = spare - addition
    return np.array([reach] + counts)


def uneven(rng, number_of, total, bound, skew):
    if number_of == 2:
        one = jax.random.randint(rng, (), max(1, total - bound), min(bound, total - 1) + 1)
        return jnp.stack([one, total - one])
    tallies = jnp.asarray(length_profile(number_of, total, bound, skew), jnp.int32)
    twos = (number_of - 1) // 2
    donor, taker = tallies[1:1 + 2 * twos:2], tallies[2:2 + 2 * twos:2]
    room = jnp.minimum(donor - 1, bound - taker)
    passed = jax.random.randint(jax.random.fold_in(rng, 1), (twos,), 0, 1 << 20) % (room + 1)
    tallies = tallies.at[1:1 + 2 * twos:2].set(donor - passed).at[2:2 + 2 * twos:2].set(taker + passed)
    return tallies[jax.random.permutation(jax.random.fold_in(rng, 2), number_of)]


def scatter_about(key, shape, scale, limit, cuts=(), held_as=jnp.bfloat16):
    drawn = jax.random.normal(key, shape, jnp.float32) * scale
    if len(cuts) > 0:
        drawn = steps_of(key, shape, cuts, -0.22, 0.18) * drawn
    return jnp.clip(drawn, min=-limit, max=limit).astype(held_as)


def setup_inputs(seed: int = 0) -> dict:
    key_of = jax.random.split(jax.random.key(seed), 16)
    return {
        "tokens": scatter_about(key_of[0], (GROUPS, GROUP, D), 1.0, 6.0, ((0, 8), (1, 4))),
        "segment_ids": jax.vmap(lambda own: jnp.searchsorted(jnp.cumsum(uneven(own, NCONT + 1, GROUP, SEG_MOST, 0)), jnp.arange(GROUP), side="right"))(jax.random.split(key_of[1], GROUPS)).reshape((GROUPS, GROUP)).astype(jnp.int32),
        "bucket_table": touch_ends(jax.random.randint(key_of[2], (GROUP,), 0, NBUCKET), jax.random.fold_in(key_of[2], 1), 0, NBUCKET - 1).astype(jnp.int32),
        "w_qkv": scatter_about(key_of[3], (D, 3 * D), D ** -0.5, 0.25, ((0, 8),)),
        "w_out": scatter_about(key_of[4], (D, D), (D // 64) ** -0.5, 2.0, ((0, 8),)),
        "w_in": scatter_about(key_of[5], (D, FF), D ** -0.5, 0.25, ((0, 8),)),
        "w_down": scatter_about(key_of[6], (FF, D), FF ** -0.5, 0.125, ((0, 8),)),
        "gain_one": jnp.clip(1.0 + 0.1 * jax.random.normal(key_of[7], (D,), jnp.float32), 0.5, 1.5).astype(jnp.bfloat16),
        "shift_one": scatter_about(key_of[8], (D,), 0.3, 1.75, ((0, 8),)),
        "gain_two": jnp.clip(1.0 + 0.1 * jax.random.normal(key_of[9], (D,), jnp.float32), 0.5, 1.5).astype(jnp.bfloat16),
        "shift_two": scatter_about(key_of[10], (D,), 0.3, 1.75, ((0, 8),)),
        "bias_in": scatter_about(key_of[11], (FF,), 0.3, 1.75, ((0, 8),)),
        "bias_down": scatter_about(key_of[12], (D,), 0.3, 1.75, ((0, 8),)),
        "rel_bias": scatter_about(key_of[13], (NBUCKET, HEADS), 1.0, 6.0),
        "cotangent": scatter_about(key_of[14], (GROUPS, GROUP, D), 1.0, 6.0, ((0, 8), (1, 4))),
    }


norm_eps = 1e-05
masked_low = -1e+30
top_precision = lax.Precision.HIGHEST

@jax.custom_vjp
def low(v):
    return lax.optimization_barrier(v.astype(jnp.bfloat16)).astype(jnp.float32)

@jax.custom_vjp
def low_back(v):
    return v

def low_keep(v):
    return (low(v), None)

def low_pass(kept, grad):
    return (grad,)

def back_keep(v):
    return (v, None)

def back_low(kept, grad):
    return (low(grad),)
low.defvjp(low_keep, low_pass)
low_back.defvjp(back_keep, back_low)

def norm_layer(features, gain_vec, shift_vec):
    centre = lax.optimization_barrier(jnp.mean(features, axis=-1, keepdims=True))
    centred = features - centre
    spread = lax.optimization_barrier(jnp.mean(centred * centred, axis=-1, keepdims=True))
    return centred * lax.rsqrt(spread + norm_eps) * gain_vec + shift_vec

def group_forward(group_tokens, seg_row, bucket_table, params):
    w_qkv, w_out, w_in, w_down, gain_one, shift_one, gain_two, shift_two, bias_in, bias_down, rel_bias = params
    row_count = group_tokens.shape[0]
    first_norm = low(norm_layer(group_tokens, gain_one, shift_one))
    packed = low(low_back(jnp.dot(first_norm, w_qkv, precision=top_precision)))
    queries = packed[:, :D].reshape(row_count, HEADS, HEAD)
    key_rows = packed[:, D:2 * D].reshape(row_count, HEADS, HEAD)
    value_rows = packed[:, 2 * D:].reshape(row_count, HEADS, HEAD)
    block_rows = min(512, row_count)
    key_pos = jnp.arange(row_count, dtype=jnp.int32)
    score_scale = HEAD ** (-0.5)

    def attend(row_start):
        query_block = lax.dynamic_slice_in_dim(queries, row_start, block_rows, 0)
        query_pos = row_start + jnp.arange(block_rows, dtype=jnp.int32)
        query_seg = lax.dynamic_slice_in_dim(seg_row, row_start, block_rows, 0)
        raw_scores = jnp.einsum('qhe,khe->hqk', query_block, key_rows, precision=top_precision)
        distance = jnp.clip(query_pos[:, None] - key_pos[None, :], 0, row_count - 1)
        bias_terms = jnp.transpose(rel_bias[bucket_table[distance]], (2, 0, 1))
        scores = low_back(raw_scores * score_scale + bias_terms)
        causal = key_pos[None, :] <= query_pos[:, None]
        shared = (seg_row[None, :] == 0) | (seg_row[None, :] == query_seg[:, None])
        allowed = causal & shared
        masked = jnp.where(allowed[None], scores, masked_low)
        row_top = lax.optimization_barrier(jnp.max(masked, axis=2, keepdims=True))
        weights = jnp.exp(masked - row_top)
        probabilities = low(weights / lax.optimization_barrier(jnp.sum(weights, axis=2, keepdims=True)))
        mixed_heads = jnp.einsum('hqk,khe->qhe', probabilities, value_rows, precision=top_precision)
        return mixed_heads.reshape(block_rows, D)
    block_starts = jnp.arange(row_count // block_rows, dtype=jnp.int32) * block_rows
    attended = lax.map(jax.checkpoint(attend), block_starts).reshape(row_count, D)
    attended = low(low_back(attended))
    mixed_out = low_back(jnp.dot(attended, w_out, precision=top_precision))
    middle = group_tokens + mixed_out
    second_norm = low(norm_layer(middle, gain_two, shift_two))
    inner_pre = low_back(jnp.dot(second_norm, w_in, precision=top_precision) + bias_in)
    activated = low(jax.nn.gelu(inner_pre, approximate=False))
    return middle + jnp.dot(activated, w_down, precision=top_precision) + bias_down

def reference(tokens, segment_ids, bucket_table, w_qkv, w_out, w_in, w_down, gain_one, shift_one, gain_two, shift_two, bias_in, bias_down, rel_bias, cotangent):
    params = tuple((weight_arg.astype(jnp.float32) for weight_arg in (w_qkv, w_out, w_in, w_down, gain_one, shift_one, gain_two, shift_two, bias_in, bias_down, rel_bias)))

    def one_group(grad_sums, group_item):
        group_tokens, seg_row, group_cot = group_item

        def forward_fn(tok_in, par_in):
            return group_forward(tok_in, seg_row, bucket_table, par_in)
        group_out, pull_back = jax.vjp(forward_fn, group_tokens.astype(jnp.float32), params)
        d_tokens, d_params = pull_back(group_cot.astype(jnp.float32))
        grad_sums = tuple((left_grad + right_grad for left_grad, right_grad in zip(grad_sums, d_params)))
        return (grad_sums, (group_out.astype(jnp.bfloat16), d_tokens.astype(jnp.bfloat16)))
    zero_grads = tuple((jnp.zeros_like(weight_arg) for weight_arg in params))
    grad_sums, (outputs, input_grads) = lax.scan(one_group, zero_grads, (tokens, segment_ids, cotangent))
    return (outputs, input_grads, grad_sums[0], grad_sums[1], grad_sums[2], grad_sums[3], grad_sums[4], grad_sums[5], grad_sums[6], grad_sums[7], grad_sums[8], grad_sums[9], grad_sums[10])
```

```python
import functools
import math
from types import SimpleNamespace

import jax
import jax.numpy as jnp
from jax import lax
from jax.experimental import pallas as pl
from jax.experimental.pallas import tpu as pltpu
from jax.sharding import PartitionSpec as P

MESH = pl.DeviceIdType.MESH
F32 = jnp.float32
BF16 = jnp.bfloat16
norm_eps = 1e-05
masked_low = -1e30
CTX = 4
LANES = 128


def mm(left, right, left_dim=1, right_dim=0):
    return lax.dot_general(
        left, right, (((left_dim,), (right_dim,)), ((), ())), preferred_element_type=F32
    )


def norm_stats(rows):
    centre = jnp.mean(rows, axis=-1, keepdims=True)
    centred = rows - centre
    spread = jnp.mean(centred * centred, axis=-1, keepdims=True)
    scale = lax.rsqrt(spread + norm_eps)
    return centred * scale, scale


def norm_back(d_normed, gain_row, hat, scale):
    d_hat = d_normed * gain_row
    mean_d = jnp.mean(d_hat, axis=-1, keepdims=True)
    mean_dh = jnp.mean(d_hat * hat, axis=-1, keepdims=True)
    return scale * (d_hat - mean_d - hat * mean_dh)


class Sizes:
    def __init__(self, n_f, rows, width, ff, group, buckets, heads):
        self.n_f = n_f
        self.half = n_f // 2
        self.rows = rows
        self.width = width
        self.ff = ff
        self.group = group
        self.buckets = buckets
        self.heads = heads
        self.head = width // heads
        self.w_rows = width // n_f
        self.d_rows = ff // n_f
        self.own_ff = ff // CTX
        self.owned = n_f // CTX
        self.blocks = CTX * (CTX + 1) // 2


class Links:
    def __init__(self, send_sems, recv_sems):
        self.send_sems = send_sems
        self.recv_sems = recv_sems
        self.used = 0
        self.pending = []

    def copy(self, src, dst, first, slot, device, index):
        return pltpu.make_async_remote_copy(
            src_ref=src,
            dst_ref=dst,
            send_sem=self.send_sems.at[index],
            recv_sem=self.recv_sems.at[first + slot],
            device_id=device,
            device_id_type=MESH,
        )

    def send(self, src, dst, first, slot, device, guard=None):
        index = self.used
        self.used += 1
        made = self.copy(src, dst, first, slot, device, index)
        if guard is None:
            made.start()
        else:
            pl.when(guard)(made.start)
        self.pending.append((made, guard))

    def wait(self, dst, first, slot, device, guard=None):
        made = self.copy(dst, dst, first, slot, device, 0)
        if guard is None:
            made.wait_recv()
        else:
            pl.when(guard)(made.wait_recv)

    def drain(self):
        for made, guard in self.pending:
            if guard is None:
                made.wait_send()
            else:
                pl.when(guard)(made.wait_send)
        self.pending = []


def count_sends(sizes):
    half, n_f = sizes.half, sizes.n_f
    weights = 3 * ((half - 1) + 1 + (half - 1)) + (half + sizes.owned // 2)
    acts = 3 + 3 + 12 + 9 + 3 + 3
    grads = 2 * (1 + half - 1 + 3) + 2 * (1 + max(1, sizes.owned // 2) + 3)
    return weights + (n_f - 1) + acts + grads + (n_f - 1) + 3 + 16


def layer_kernel(
    sizes,
    tok_in,
    seg_in,
    table_in,
    wqkv_in,
    wout_in,
    win_in,
    wdown_in,
    vec_in0,
    vec_in1,
    vec_in2,
    vec_in3,
    vec_in4,
    bias_in_in,
    rel_in,
    dy_in,
    out_ref,
    dx_ref,
    gqkv_ref,
    gout_ref,
    gin_ref,
    gdown_ref,
    small_ref,
    *scratch_refs,
):
    s, sem = name_scratch(scratch_spec(sizes), scratch_refs[:-3])
    send_sems, recv_sems, own_sems = scratch_refs[-3:]
    n_f, half, rows = sizes.n_f, sizes.half, sizes.rows
    width, w_rows, d_rows, own_ff = sizes.width, sizes.w_rows, sizes.d_rows, sizes.own_ff
    owned = sizes.owned
    head = sizes.head

    c = lax.axis_index("ctx")
    f = lax.axis_index("fsdp")
    side = c // 2
    core = c % 2
    place = f // 2
    par = f % 2
    sib = side * 2 + 1 - core
    opp = (1 - side) * 2 + core
    diag = (1 - side) * 2 + 1 - core
    first_owned = c * owned
    is_owner = (f // owned) == c
    own_slot = f % owned

    def ctx_dev(index):
        return {"ctx": index, "fsdp": f}

    def f_dev(index):
        return {"ctx": c, "fsdp": index}

    partner = 2 * place + 1 - par

    def other_place(step):
        return lax.rem(place + step, half)

    links = Links(send_sems, recv_sems)

    barrier = pltpu.get_barrier_semaphore()
    for step in range(1, CTX):
        pl.semaphore_signal(
            barrier, inc=1, device_id=ctx_dev(lax.rem(c + step, CTX)), device_id_type=MESH
        )
    for step in range(1, n_f):
        pl.semaphore_signal(
            barrier, inc=1, device_id=f_dev(lax.rem(f + step, n_f)), device_id_type=MESH
        )

    own_copies = []

    def fetch(src, dst):
        made = pltpu.make_async_copy(src, dst, own_sems.at[len(own_copies)])
        own_copies.append(made)
        made.start()
        return made

    first_fetches = []
    for part in range(3):
        cols = pl.ds(pl.multiple_of(part * width + c * LANES, LANES), LANES)
        first_fetches.append(
            fetch(wqkv_in.at[:, cols], s.wq.at[f, :, part * LANES : (part + 1) * LANES])
        )
    first_fetches.append(fetch(tok_in, s.tok.at[c]))
    own_cols = pl.ds(pl.multiple_of(c * own_ff, own_ff), own_ff)
    later_fetches = [
        fetch(wout_in, s.wo.at[f]),
        fetch(win_in.at[:, own_cols], s.wi.at[f]),
        fetch(dy_in, s.dy.at[c]),
    ]
    down_fetch = pltpu.make_async_copy(
        wdown_in, s.wd.at[own_slot], own_sems.at[len(own_copies)]
    )
    pl.when(is_owner)(down_fetch.start)
    for at, ref in enumerate((vec_in0, vec_in1, vec_in2, vec_in3, vec_in4)):
        s.vec[f, at : at + 1, 0:w_rows] = ref[...].astype(F32)
    for at in range(bias_in_in.shape[0]):
        size = bias_in_in.shape[1]
        s.vec[f, 5:6, at * size : (at + 1) * size] = bias_in_in[at : at + 1, :].astype(F32)
    for made in first_fetches:
        made.wait()

    pl.semaphore_wait(barrier, CTX - 1 + n_f - 1)

    for step in range(1, n_f):
        to = lax.rem(f + step, n_f)
        links.send(s.vec.at[f], s.vec.at[f], sem.vec, f, f_dev(to))

    def spread(buf, first):
        for step in range(1, half):
            links.send(buf.at[f], buf.at[f], first, f, f_dev(2 * other_place(step) + par))
        links.send(buf.at[f], buf.at[f], first, f, f_dev(partner))

    def pass_on(buf, first):
        for step in range(1, half):
            src = 2 * other_place(step) + par
            links.wait(buf.at[src], first, src, f_dev(src))
            links.send(buf.at[src], buf.at[src], first, src, f_dev(partner))

    def settle(buf, first):
        for step in range(half):
            src = 2 * other_place(step) + 1 - par
            links.wait(buf.at[src], first, src, f_dev(partner))

    spread(s.wq, sem.wq)
    for to in (sib, opp):
        links.send(s.tok.at[c], s.tok.at[c], sem.tok, c, ctx_dev(to))

    ids = lax.broadcasted_iota(jnp.int32, (sizes.buckets, sizes.group), 0)
    onehot = (ids == table_in[...]).astype(BF16)
    s.hot[...] = onehot.astype(F32)
    s.bvec[...] = mm(rel_in[...], onehot)
    for h in range(2):
        row = s.bvec[pl.ds(2 * c + h, 1), :]
        for delta in range(CTX):
            now = row[:, delta * rows : (delta + 1) * rows]
            before = row[:, (delta - 1) * rows : delta * rows] if delta else now
            wide = jnp.broadcast_to(jnp.concatenate([now, before], axis=1), (rows, 2 * rows))
            turned = pltpu.roll(wide, 0, 1, stride=1, stride_axis=0)
            s.tile[h, delta] = turned[:, :rows]
    seg_f = seg_in[...].astype(F32)
    for at in range(CTX):
        piece = jnp.broadcast_to(seg_f[:, at * rows : (at + 1) * rows], (rows, rows))
        s.segk[at] = jnp.transpose(piece)
    key_pos = lax.broadcasted_iota(jnp.int32, (rows, rows), 0)
    query_pos = lax.broadcasted_iota(jnp.int32, (rows, rows), 1)
    for q_at in range(CTX):
        seg_q = jnp.broadcast_to(seg_f[:, q_at * rows : (q_at + 1) * rows], (rows, rows))
        for k_at in range(q_at + 1):
            seg_k = s.segk[k_at]
            allowed = (seg_k == 0.0) | (seg_k == seg_q)
            if q_at == k_at:
                allowed = allowed & (key_pos <= query_pos)
            for h in range(2):
                block = q_at * (q_at + 1) // 2 + k_at
                s.bm[h, block] = jnp.where(allowed, s.tile[h, q_at - k_at], masked_low)

    for step in range(1, n_f):
        src = lax.rem(f + step, n_f)
        links.wait(s.vec.at[src], sem.vec, src, f_dev(src))

    def joined(pieces, count, size):
        total = count * size
        spot = lax.broadcasted_iota(jnp.int32, (size, total), 1) % size
        which = lax.broadcasted_iota(jnp.int32, (size, total), 0)
        spreader = (spot == which).astype(BF16)
        flat = mm(pieces.astype(BF16), spreader)
        owner = lax.broadcasted_iota(jnp.int32, (count, total), 1) // size
        mine = owner == lax.broadcasted_iota(jnp.int32, (count, total), 0)
        return jnp.sum(jnp.where(mine, flat, 0.0), axis=0, keepdims=True)

    for at in range(5):
        s.vrow[at : at + 1, :] = joined(s.vec[:, at, 0:w_rows], n_f, w_rows)
    s.vrow[5:6, :] = joined(s.vec[pl.ds(first_owned, owned), 5, 0:d_rows], owned, d_rows)
    gain_one, shift_one = s.vrow[0:1, :], s.vrow[1:2, :]
    gain_two, shift_two = s.vrow[2:3, :], s.vrow[3:4, :]
    bias_down_row, bias_in_row = s.vrow[4:5, :], s.vrow[5:6, :]

    step_rows = 64

    def row_loop(body, count=rows):
        def run(at, carried):
            body(pl.ds(pl.multiple_of(at * step_rows, step_rows), step_rows))
            return carried

        lax.fori_loop(0, count // step_rows, run, 0)

    def first_norm(chunk):
        def body(part):
            hat, scale = norm_stats(s.tok[chunk, part, :].astype(F32))
            s.fn[chunk, part, :] = (hat * gain_one + shift_one).astype(BF16)

        row_loop(body)

    def whole(buf, count, size, kept):
        if size % 16 == 0:
            return buf[...].reshape(count * size, buf.shape[2])
        for at in range(count):
            kept[at * size : (at + 1) * size, :] = buf[at]
        return kept[...]

    head_rows = lax.broadcasted_iota(jnp.int32, (LANES, rows), 0) // head

    def project(chunk):
        weights = whole(s.wq, n_f, w_rows, s.flat_wq)
        made = mm(s.fn[chunk], weights)
        queries = made[:, 0:LANES].astype(BF16).astype(F32) * (head ** -0.5)
        keys = made[:, LANES : 2 * LANES]
        values = made[:, 2 * LANES : 3 * LANES]
        s.k[chunk] = keys.astype(BF16)
        s.v[chunk] = values.astype(BF16)
        s.kt[chunk] = jnp.transpose(keys).astype(BF16)
        s.vt[chunk] = jnp.transpose(values).astype(BF16)
        turned = jnp.transpose(queries)
        for h in range(2):
            kept = jnp.where(head_rows == h, turned, 0.0)
            s.qt[h, chunk] = kept.astype(BF16)
            s.q[h, chunk] = jnp.transpose(kept).astype(BF16)

    first_norm(c)
    pass_on(s.wq, sem.wq)
    links.wait(s.tok.at[sib], sem.tok, sib, ctx_dev(sib))
    first_norm(sib)
    links.wait(s.tok.at[opp], sem.tok, opp, ctx_dev(opp))
    links.send(s.tok.at[opp], s.tok.at[opp], sem.tok, opp, ctx_dev(sib))
    first_norm(opp)

    for made in later_fetches:
        made.wait()
    pl.when(is_owner)(down_fetch.wait)
    spread(s.wo, sem.wo)
    spread(s.wi, sem.wi)
    down_src = s.wd.at[own_slot]
    for step in range(1, half):
        to = 2 * other_place(step) + par
        links.send(down_src, down_src, sem.wd, own_slot, f_dev(to), is_owner)
    links.send(down_src, down_src, sem.wd, own_slot, f_dev(partner), is_owner)
    for to in (sib, opp):
        links.send(s.dy.at[c], s.dy.at[c], sem.dy, c, ctx_dev(to))

    settle(s.wq, sem.wq)
    project(c)
    project(sib)
    project(opp)
    links.wait(s.tok.at[diag], sem.tok, diag, ctx_dev(sib))
    first_norm(diag)
    project(diag)

    def attend(chunk):
        first_block = chunk * (chunk + 1) // 2

        def score_pass(k_at, tops):
            keys = s.k[k_at]
            grown = []
            for h in range(2):
                scores = mm(keys, s.qt[h, chunk]) + s.bm[h, first_block + k_at]
                s.sc[h, k_at] = scores
                grown.append(jnp.maximum(tops[h], jnp.max(scores, axis=0, keepdims=True)))
            return tuple(grown)

        low = jnp.full((1, rows), masked_low, F32)
        tops = lax.fori_loop(0, chunk + 1, score_pass, (low, low))
        s.acc[...] = jnp.zeros((LANES, rows), F32)

        def value_pass(k_at, sums):
            grown = []
            for h in range(2):
                weights = jnp.exp(s.sc[h, k_at] - tops[h])
                grown.append(sums[h] + jnp.sum(weights, axis=0, keepdims=True))
                rounded = weights.astype(BF16)
                s.e[h, first_block + k_at] = rounded
                part = slice(h * head, (h + 1) * head)
                s.acc[part, :] += mm(s.vt[k_at, part, :], rounded)
            return tuple(grown)

        none = jnp.zeros((1, rows), F32)
        sums = lax.fori_loop(0, chunk + 1, value_pass, (none, none))
        for h in range(2):
            part = slice(h * head, (h + 1) * head)
            inverse = 1.0 / sums[h]
            s.linv[chunk, h : h + 1, :] = inverse
            s.att_t[chunk, part, :] = s.acc[part, :] * inverse
        s.att[c, chunk] = jnp.transpose(s.att_t[chunk]).astype(BF16)

    def att_slot(owner, chunk):
        return owner * CTX + chunk

    def send_att(chunk):
        piece = s.att.at[c, chunk]
        for to in (sib, opp):
            links.send(piece, piece, sem.att, att_slot(c, chunk), ctx_dev(to))

    def wait_att(owner, chunk, via):
        links.wait(s.att.at[owner, chunk], sem.att, att_slot(owner, chunk), ctx_dev(via))

    def pass_att(chunk):
        wait_att(opp, chunk, opp)
        piece = s.att.at[opp, chunk]
        links.send(piece, piece, sem.att, att_slot(opp, chunk), ctx_dev(sib))

    mine = [lax.rem(2 * side + step, CTX) for step in range(CTX)]
    theirs = [lax.rem(2 * (1 - side) + step, CTX) for step in range(CTX)]
    attend(mine[0])
    send_att(mine[0])
    pass_on(s.wo, sem.wo)
    attend(mine[1])
    send_att(mine[1])
    pass_on(s.wi, sem.wi)
    pass_att(theirs[0])
    links.wait(s.dy.at[opp], sem.dy, opp, ctx_dev(opp))
    links.send(s.dy.at[opp], s.dy.at[opp], sem.dy, opp, ctx_dev(sib))
    attend(mine[2])
    send_att(mine[2])
    pass_att(theirs[1])
    for at in range(owned // 2):
        slot = 2 * at + par
        src = first_owned + slot
        away = src != f
        links.wait(s.wd.at[slot], sem.wd, slot, f_dev(src), away)
        links.send(s.wd.at[slot], s.wd.at[slot], sem.wd, slot, f_dev(partner), away)
    attend(mine[3])
    send_att(mine[3])

    settle(s.wo, sem.wo)
    settle(s.wi, sem.wi)
    for at in range(owned // 2):
        slot = 2 * at + 1 - par
        links.wait(s.wd.at[slot], sem.wd, slot, f_dev(partner))
    links.wait(s.dy.at[sib], sem.dy, sib, ctx_dev(sib))
    links.wait(s.dy.at[diag], sem.dy, diag, ctx_dev(sib))
    pass_att(theirs[2])
    pass_att(theirs[3])
    seen = {}

    def gather_att(chunk):
        wait_att(sib, chunk, sib)
        wait_att(diag, chunk, sib)

    def feed(chunk, own):
        gather_att(chunk)
        w_out = whole(s.wo, n_f, w_rows, s.flat_wo)
        mixed = jnp.zeros((rows, width), F32)
        for owner in range(CTX):
            mixed += mm(s.att[owner, chunk], w_out[owner * LANES : (owner + 1) * LANES, :])
        s.mid[...] = mixed + s.tok[chunk].astype(F32)

        def normed(part):
            hat, scale = norm_stats(s.mid[part, :])
            s.sn[chunk, part, :] = (hat * gain_two + shift_two).astype(BF16)

        row_loop(normed)
        w_in = whole(s.wi, n_f, w_rows, s.flat_wi)
        w_down = whole(s.wd, owned, d_rows, None)
        s.inner[...] = mm(s.sn[chunk], w_in)
        s.dact[...] = mm(s.dy[chunk], w_down, 1, 1)

        def gelu(part):
            inner = s.inner[part, :] + bias_in_row
            phi = 0.5 + 0.5 * lax.erf(inner * (2.0 ** -0.5))
            slope = phi + inner * (jnp.exp(-0.5 * inner * inner) * (1.0 / math.sqrt(2.0 * math.pi)))
            s.actv[chunk, part, :] = (inner * phi).astype(BF16)
            s.din[chunk, part, :] = (s.dact[part, :] * slope).astype(BF16)

        row_loop(gelu)
        return mm(s.din[chunk], w_in, 1, 1)

    def scatter_first(group, first, part):
        group[0][...] = part.astype(BF16)
        links.send(group[0], group[1], first[0], 0, ctx_dev(sib))

    def scatter_second(group, first, part):
        links.wait(group[1], first[0], 0, ctx_dev(sib))
        group[2][...] = (part + group[1][...].astype(F32)).astype(BF16)
        links.send(group[2], group[3], first[1], 0, ctx_dev(opp))

    def scatter_third(group, first, part):
        group[4][...] = part.astype(BF16)
        links.send(group[4], group[5], first[2], 0, ctx_dev(sib))

    def scatter_wait(group, first):
        links.wait(group[5], first[2], 0, ctx_dev(sib))
        links.wait(group[3], first[1], 0, ctx_dev(opp))

    def scatter_sum(group, part):
        return group[3][part, :].astype(F32) + group[5][part, :].astype(F32)

    scatter_first(s.rs_s, sem.rs_s, feed(diag, False))
    scatter_second(s.rs_s, sem.rs_s, feed(opp, False))
    scatter_third(s.rs_s, sem.rs_s, feed(sib, False))
    s.dsec[...] = feed(c, True)

    w_down = whole(s.wd, owned, d_rows, None)
    scatter_first(s.rs_o, sem.rs_o, mm(s.actv[diag], w_down))
    scatter_second(s.rs_o, sem.rs_o, mm(s.actv[opp], w_down))
    scatter_third(s.rs_o, sem.rs_o, mm(s.actv[sib], w_down))
    s.outp[...] = s.mid[...] + mm(s.actv[c], w_down) + bias_down_row

    def even_pieces(group, left, right, cols):
        for at in range(width // LANES):
            lhs = left[:, :, at * LANES : (at + 1) * LANES].reshape(CTX * rows, LANES)
            made = mm(lhs, right[...].reshape(CTX * rows, cols), 0, 0).astype(BF16)
            for piece in range(LANES // w_rows):
                to = at * (LANES // w_rows) + piece
                group[0][to % 2, to // 2] = made[piece * w_rows : (piece + 1) * w_rows, :]

    def grad_pair(group, first):
        links.send(
            group[0].at[1 - par], group[1], first[0], 0, f_dev(partner)
        )

    def grad_even_second(group, first):
        links.wait(group[1], first[0], 0, f_dev(partner))
        group[2][...] = (
            group[0][par].astype(F32) + group[1][...].astype(F32)
        ).astype(BF16)
        for step in range(1, half):
            to = other_place(step)
            links.send(
                group[2].at[to], group[3].at[place], first[1], place, f_dev(2 * to + par)
            )

    def grad_even_third(group, first):
        total = group[2][place].astype(F32)
        for step in range(1, half):
            src = other_place(step)
            links.wait(group[3].at[src], first[1], src, f_dev(2 * src + par))
            total += group[3][src].astype(F32)
        group[4][c] = total.astype(BF16)
        for step in range(1, CTX):
            to = lax.rem(c + step, CTX)
            links.send(group[4].at[c], group[4].at[c], first[2], c, ctx_dev(to))

    def grad_even_wait(group, first):
        for step in range(1, CTX):
            src = lax.rem(c + step, CTX)
            links.wait(group[4].at[src], first[2], src, ctx_dev(src))

    own_half = owned // 2

    def grad_odd_second(group, first):
        links.wait(group[1], first[0], 0, f_dev(partner))
        group[2][...] = (
            group[0][par].astype(F32) + group[1][...].astype(F32)
        ).astype(BF16)
        for at in range(own_half):
            to = c * own_half + at
            links.send(
                group[2].at[at],
                group[3].at[place],
                first[1],
                place,
                f_dev(2 * to + par),
                to != place,
            )

    owner_ctx = f // owned

    def grad_odd_third(group, first):
        for step in range(1, half):
            src = other_place(step)
            links.wait(group[3].at[src], first[1], src, f_dev(2 * src + par), is_owner)

        @pl.when(is_owner)
        def add_up():
            total = group[2][lax.rem(place, own_half)].astype(F32)
            for step in range(1, half):
                total += group[3][other_place(step)].astype(F32)
            group[4][...] = total.astype(BF16)

        for step in range(1, CTX):
            to = lax.rem(c + step, CTX)
            links.send(group[4], group[4], first[2], 0, ctx_dev(to), is_owner)

    def grad_odd_wait(group, first):
        links.wait(group[4], first[2], 0, ctx_dev(owner_ctx), jnp.logical_not(is_owner))

    def down_pieces():
        for at in range(own_ff // LANES):
            lhs = s.actv[:, :, at * LANES : (at + 1) * LANES].reshape(CTX * rows, LANES)
            made = mm(lhs, s.dy[...].reshape(CTX * rows, width), 0, 0).astype(BF16)
            low, high = at * LANES, (at + 1) * LANES
            for slot in range(owned):
                left, right = max(low, slot * d_rows), min(high, (slot + 1) * d_rows)
                if left < right:
                    inside = slice(left - slot * d_rows, right - slot * d_rows)
                    s.gd[0][slot % 2, slot // 2, inside, :] = made[left - low : right - low, :]

    down_pieces()
    grad_pair(s.gd, sem.gd)
    even_pieces(s.gi, s.sn, s.din, own_ff)
    grad_pair(s.gi, sem.gi)

    scatter_wait(s.rs_s, sem.rs_s)

    def zero_sums():
        s.vg[...] = jnp.zeros_like(s.vg)

    zero_sums()

    def second_back(part):
        hat, scale = norm_stats(s.mid[part, :])
        d_second = s.dsec[part, :] + scatter_sum(s.rs_s, part)
        d_result = s.dy[c, part, :].astype(F32)
        d_middle = d_result + norm_back(d_second, gain_two, hat, scale)
        s.dmid[part, :] = d_middle
        s.dmx[c, part, :] = d_middle.astype(BF16)
        s.vg[2:3, :] += jnp.sum(d_second * hat, axis=0, keepdims=True)
        s.vg[3:4, :] += jnp.sum(d_second, axis=0, keepdims=True)
        s.vg[4:5, :] += jnp.sum(d_result, axis=0, keepdims=True)

    row_loop(second_back)
    d_att = mm(whole(s.wo, n_f, w_rows, s.flat_wo), s.dmx[c], 1, 1)
    s.dat_out[...] = d_att.astype(BF16).reshape(CTX, LANES, rows)
    for to in (opp, diag, sib):
        links.send(s.dat_out.at[to], s.dat.at[c], sem.dat, c, ctx_dev(to))
    s.dat[c] = s.dat_out[c]
    for to in (sib, opp):
        links.send(s.dmx.at[c], s.dmx.at[c], sem.dmx, c, ctx_dev(to))
    grad_even_second(s.gi, sem.gi)
    grad_odd_second(s.gd, sem.gd)
    for at in range(CTX):
        def bias_rows(part, at=at):
            s.vg[5:6, :] += jnp.sum(s.din[at, part, :].astype(F32), axis=0, keepdims=True)

        row_loop(bias_rows)
    scatter_wait(s.rs_o, sem.rs_o)
    out_ref[...] = (
        s.outp[...] + s.rs_o[3][...].astype(F32) + s.rs_o[5][...].astype(F32)
    ).astype(BF16)

    for src in (sib, opp, diag):
        links.wait(s.dat.at[src], sem.dat, src, ctx_dev(src))
    for at in range(CTX):
        got = s.dat[at].astype(F32)
        for h in range(2):
            part = slice(h * head, (h + 1) * head)
            scaled = (got * s.linv[at, h : h + 1, :]).astype(BF16)
            kept = jnp.where(head_rows == h, scaled.astype(F32), 0.0)
            s.dat_t[h, at] = kept.astype(BF16)
            s.dat_n[h, at] = jnp.transpose(kept).astype(BF16)
            s.delta[at, h : h + 1, :] = jnp.sum(
                kept[part, :] * s.att_t[at, part, :], axis=0, keepdims=True
            )
        s.dqt[at] = jnp.zeros((LANES, rows), F32)
    s.dbm[...] = jnp.zeros_like(s.dbm)

    def key_block(k_at, carried):
        s.dk[...] = jnp.zeros((rows, LANES), F32)
        s.dv[...] = jnp.zeros((rows, LANES), F32)

        def query_block(q_at, inner_carried):
            block = q_at * (q_at + 1) // 2 + k_at
            values = s.v[k_at]
            for h in range(2):
                part = slice(h * head, (h + 1) * head)
                d_probs = mm(values, s.dat_t[h, q_at])
                rounded = s.e[h, block]
                d_scores = rounded.astype(F32) * (d_probs - s.delta[q_at, h : h + 1, :])
                s.dbm[h, q_at - k_at] += d_scores
                low = d_scores.astype(BF16)
                s.dk[...] += mm(low, s.q[h, q_at])
                s.dv[...] += mm(rounded, s.dat_n[h, q_at])
                s.dqt[q_at, part, :] += mm(s.kt[k_at, part, :], low)
            return inner_carried

        lax.fori_loop(k_at, CTX, query_block, 0)
        s.dp[k_at, :, LANES : 2 * LANES] = s.dk[...].astype(BF16)
        s.dp[k_at, :, 2 * LANES : 3 * LANES] = s.dv[...].astype(BF16)
        return carried

    lax.fori_loop(0, CTX, key_block, 0)
    for at in range(CTX):
        s.dp[at, :, 0:LANES] = (jnp.transpose(s.dqt[at]) * (head ** -0.5)).astype(BF16)

    w_qkv = whole(s.wq, n_f, w_rows, s.flat_wq)
    scatter_first(s.rs_f, sem.rs_f, mm(s.dp[diag], w_qkv, 1, 1))
    scatter_second(s.rs_f, sem.rs_f, mm(s.dp[opp], w_qkv, 1, 1))
    even_pieces(s.gq, s.fn, s.dp, 3 * LANES)
    grad_pair(s.gq, sem.gq)
    scatter_third(s.rs_f, sem.rs_f, mm(s.dp[sib], w_qkv, 1, 1))
    s.dsec[...] = mm(s.dp[c], w_qkv, 1, 1)

    links.wait(s.dmx.at[opp], sem.dmx, opp, ctx_dev(opp))
    links.send(s.dmx.at[opp], s.dmx.at[opp], sem.dmx, opp, ctx_dev(sib))
    grad_even_third(s.gi, sem.gi)
    grad_odd_third(s.gd, sem.gd)
    grad_even_second(s.gq, sem.gq)
    links.wait(s.dmx.at[sib], sem.dmx, sib, ctx_dev(sib))
    links.wait(s.dmx.at[diag], sem.dmx, diag, ctx_dev(sib))
    made = jnp.zeros((LANES, width), F32)
    for at in range(CTX):
        made += mm(s.att_t[at].astype(BF16), s.dmx[at])
    for slot in range(owned):
        s.go[0][slot % 2, slot // 2] = made[slot * w_rows : (slot + 1) * w_rows, :].astype(BF16)
    grad_pair(s.go, sem.go)

    for h in range(2):
        pieces = []
        for delta in range(CTX):
            block = s.dbm[h, delta]
            wide = jnp.concatenate([block, jnp.zeros((rows, rows), F32)], axis=1)
            count = rows
            while count > 1:
                count //= 2
                turned = pltpu.roll(wide[count : 2 * count, :], 2 * rows - count, 1)
                wide = wide[0:count, :] + turned
            pieces.append(wide)
        total = []
        for delta in range(CTX):
            here = pieces[delta][:, 0:rows]
            if delta + 1 < CTX:
                here = here + pieces[delta + 1][:, rows : 2 * rows]
            total.append(here)
        dist = jnp.concatenate(total, axis=1)
        sums = lax.dot_general(
            jnp.broadcast_to(dist, (8, sizes.group)),
            s.hot[...],
            (((1,), (1,)), ((), ())),
            preferred_element_type=F32,
            precision=lax.Precision.HIGHEST,
        )
        line = lax.broadcasted_iota(jnp.int32, sums.shape, 0)
        s.vg[8:16, 0 : sizes.buckets] += jnp.where(line == 2 * c + h, sums, 0.0)

    scatter_wait(s.rs_f, sem.rs_f)

    def first_back(part):
        hat, scale = norm_stats(s.tok[c, part, :].astype(F32))
        d_first = s.dsec[part, :] + scatter_sum(s.rs_f, part)
        d_x = s.dmid[part, :] + norm_back(d_first, gain_one, hat, scale)
        dx_ref[part, :] = d_x.astype(BF16)
        s.vg[0:1, :] += jnp.sum(d_first * hat, axis=0, keepdims=True)
        s.vg[1:2, :] += jnp.sum(d_first, axis=0, keepdims=True)

    row_loop(first_back)
    s.vgf[f] = s.vg[...]
    for step in range(1, n_f):
        to = lax.rem(f + step, n_f)
        links.send(s.vg, s.vgf.at[f], sem.vgf, f, f_dev(to))
    grad_odd_second(s.go, sem.go)
    grad_even_third(s.gq, sem.gq)
    for step in range(1, n_f):
        src = lax.rem(f + step, n_f)
        links.wait(s.vgf.at[src], sem.vgf, src, f_dev(src))
    s.vgc[c] = jnp.sum(s.vgf[...], axis=0)
    for step in range(1, CTX):
        to = lax.rem(c + step, CTX)
        links.send(s.vgc.at[c], s.vgc.at[c], sem.vgc, c, ctx_dev(to))
    grad_odd_third(s.go, sem.go)

    grad_even_wait(s.gi, sem.gi)
    gin_ref[...] = s.gi[4][...]
    grad_odd_wait(s.gd, sem.gd)
    gdown_ref[...] = s.gd[4][...]
    grad_even_wait(s.gq, sem.gq)
    gqkv_ref[...] = s.gq[4][...]
    grad_odd_wait(s.go, sem.go)
    gout_ref[...] = s.go[4][...]
    for step in range(1, CTX):
        src = lax.rem(c + step, CTX)
        links.wait(s.vgc.at[src], sem.vgc, src, ctx_dev(src))
    total = jnp.sum(s.vgc[...], axis=0)
    small_ref[0:8, :] = pltpu.roll(total[0:8, :], lax.rem(width - f * w_rows, width), 1)
    hidden = pltpu.roll(s.vgc[owner_ctx, 0:8, :], lax.rem(own_ff - own_slot * d_rows, own_ff), 1)
    small_ref[5:6, :] = hidden[5:6, :]
    small_ref[8:16, :] = total[8:16, :]
    links.drain()


def finish_kernel(
    sizes,
    out_in,
    dx_in,
    gqkv_in,
    gout_in,
    gin_in,
    gdown_in,
    small_in,
    out_ref,
    dx_ref,
    gqkv_ref,
    gout_ref,
    gin_ref,
    gdown_ref,
    gg1_ref,
    gs1_ref,
    gg2_ref,
    gs2_ref,
    gbi_ref,
    gbd_ref,
    grel_ref,
    gqkv,
    gout,
    gin,
    gdown,
    gqkv_low,
    gout_low,
    gin_low,
    gdown_low,
    out_low,
    dx_low,
    sems,
):
    made = []

    def start(src, dst):
        copy = pltpu.make_async_copy(src, dst, sems.at[len(made)])
        copy.start()
        made.append(copy)
        return copy

    loads = [
        start(gdown_in, gdown_low),
        start(gin_in, gin_low),
        start(gqkv_in, gqkv_low),
        start(gout_in, gout_low),
    ]
    loads += [start(out_in, out_low), start(dx_in, dx_low)]
    width, own_ff = sizes.width, sizes.own_ff
    loads[0].wait()
    gdown[...] = gdown_low[...].astype(F32)
    stores = [start(gdown, gdown_ref)]
    loads[1].wait()
    for at in range(CTX):
        gin[:, at * own_ff : (at + 1) * own_ff] = gin_low[at].astype(F32)
    stores.append(start(gin, gin_ref))
    loads[2].wait()
    for at in range(CTX):
        for part in range(3):
            low = part * width + at * LANES
            gqkv[:, low : low + LANES] = gqkv_low[at, :, part * LANES : (part + 1) * LANES].astype(F32)
    stores.append(start(gqkv, gqkv_ref))
    loads[3].wait()
    gout[...] = gout_low[...].astype(F32)
    stores.append(start(gout, gout_ref))
    loads[4].wait()
    stores.append(start(out_low, out_ref))
    loads[5].wait()
    stores.append(start(dx_low, dx_ref))
    for at, ref in enumerate((gg1_ref, gs1_ref, gg2_ref, gs2_ref, gbd_ref)):
        ref[...] = small_in[at : at + 1, 0 : sizes.w_rows]
    size = gbi_ref.shape[1]
    for at in range(gbi_ref.shape[0]):
        gbi_ref[at : at + 1, :] = small_in[5:6, at * size : (at + 1) * size]
    grel_ref[...] = small_in[8:16, 0 : sizes.buckets]
    for copy in stores:
        copy.wait()


def scratch_spec(z):
    rows, width, group = z.rows, z.width, z.group
    own_half = z.owned // 2
    blocks = CTX * (CTX + 1) // 2
    act = (CTX, rows, width)
    hidden = (CTX, rows, z.own_ff)
    tall = (CTX, rows, LANES)
    wide = (CTX, LANES, rows)
    squares = (2, CTX, rows, rows)

    def scatter():
        flat = ((rows, width), BF16)
        landing = ((rows, width), BF16, 1)
        return [flat, landing, flat, landing, flat, landing]

    def even(cols):
        part = (z.half, z.w_rows, cols)
        return [
            ((2,) + part, BF16),
            (part, BF16, 1),
            (part, BF16),
            (part, BF16, z.half),
            ((CTX, z.w_rows, cols), BF16, CTX),
        ]

    def odd(size):
        part = (own_half, size, width)
        return [
            ((2,) + part, BF16),
            (part, BF16, 1),
            (part, BF16),
            ((z.half, size, width), BF16, z.half),
            ((size, width), BF16, 1),
        ]

    spec = dict(
        tok=(act, BF16, CTX),
        dy=(act, BF16, CTX),
        fn=(act, BF16),
        wq=((z.n_f, z.w_rows, 3 * LANES), BF16, z.n_f),
        wo=((z.n_f, z.w_rows, width), BF16, z.n_f),
        wi=((z.n_f, z.w_rows, z.own_ff), BF16, z.n_f),
        wd=((z.owned, z.d_rows, width), BF16, z.owned),
        vec=((z.n_f, 8, max(z.d_rows, LANES)), F32, z.n_f),
        vrow=((8, width), F32),
        hot=((z.buckets, group), F32),
        bvec=((8, group), F32),
        tile=(squares, F32),
        segk=((CTX, rows, rows), F32),
        bm=((2, blocks, rows, rows), F32),
        k=(tall, BF16),
        v=(tall, BF16),
        kt=(wide, BF16),
        vt=(wide, BF16),
        qt=((2,) + wide, BF16),
        q=((2,) + tall, BF16),
        sc=(squares, F32),
        e=((2, blocks, rows, rows), BF16),
        acc=((LANES, rows), F32),
        linv=((CTX, 8, rows), F32),
        att_t=(wide, F32),
        att=((CTX,) + tall, BF16, CTX * CTX),
        mid=((rows, width), F32),
        sn=(act, BF16),
        inner=((rows, z.own_ff), F32),
        dact=((rows, z.own_ff), F32),
        actv=(hidden, BF16),
        din=(hidden, BF16),
        dsec=((rows, width), F32),
        outp=((rows, width), F32),
        dmid=((rows, width), F32),
        dmx=(act, BF16, CTX),
        dat_out=(wide, BF16),
        dat=(wide, BF16, CTX),
        dat_t=((2,) + wide, BF16),
        dat_n=((2,) + tall, BF16),
        delta=((CTX, 8, rows), F32),
        dqt=(wide, F32),
        dbm=(squares, F32),
        dk=((rows, LANES), F32),
        dv=((rows, LANES), F32),
        dp=((CTX, rows, 3 * LANES), BF16),
        vg=((16, width), F32),
        vgf=((z.n_f, 16, width), F32, z.n_f),
        vgc=((CTX, 16, width), F32, CTX),
        rs_s=scatter(),
        rs_o=scatter(),
        rs_f=scatter(),
        gq=even(3 * LANES),
        gi=even(z.own_ff),
        go=odd(z.w_rows),
        gd=odd(z.d_rows),
    )
    if z.w_rows % 16:
        spec.update(
            flat_wq=((width, 3 * LANES), BF16),
            flat_wo=((width, width), BF16),
            flat_wi=((width, z.own_ff), BF16),
        )
    else:
        spec.update(flat_wq=((8, LANES), BF16), flat_wo=((8, LANES), BF16), flat_wi=((8, LANES), BF16))
    return spec


def scratch_items(spec):
    for item in spec.values():
        if isinstance(item, list):
            yield from item
        else:
            yield item


def name_scratch(spec, refs):
    refs = iter(refs)
    by_name, first, used = {}, {}, 0
    for name, item in spec.items():
        entries = item if isinstance(item, list) else [item]
        held, starts = [], []
        for entry in entries:
            held.append(next(refs))
            if len(entry) > 2:
                starts.append(used)
                used += entry[2]
        by_name[name] = held if isinstance(item, list) else held[0]
        if starts:
            first[name] = starts if isinstance(item, list) else starts[0]
    return SimpleNamespace(**by_name), SimpleNamespace(**first)


def per_device(
    n_f,
    tokens,
    segment_ids,
    bucket_table,
    w_qkv,
    w_out,
    w_in,
    w_down,
    gain_one,
    shift_one,
    gain_two,
    shift_two,
    bias_in,
    bias_down,
    rel_bias,
    cotangent,
):
    sizes = Sizes(
        n_f,
        tokens.shape[1],
        tokens.shape[2],
        w_in.shape[1],
        segment_ids.shape[1],
        rel_bias.shape[0],
        rel_bias.shape[1],
    )
    rows, width, w_rows, d_rows = sizes.rows, sizes.width, sizes.w_rows, sizes.d_rows
    vmem = pl.BlockSpec(memory_space=pltpu.VMEM)
    far = pl.BlockSpec(memory_space=pltpu.HBM)
    spec = scratch_spec(sizes)
    n_recv = sum(item[2] for item in scratch_items(spec) if len(item) > 2)
    bias_shape = (max(1, d_rows // LANES), min(LANES, d_rows))
    shaped = jax.ShapeDtypeStruct
    made = pl.pallas_call(
        functools.partial(layer_kernel, sizes),
        out_shape=[
            shaped((rows, width), BF16),
            shaped((rows, width), BF16),
            shaped((CTX, w_rows, 3 * LANES), BF16),
            shaped((w_rows, width), BF16),
            shaped((CTX, w_rows, sizes.own_ff), BF16),
            shaped((d_rows, width), BF16),
            shaped((16, width), F32),
        ],
        in_specs=[far, vmem, vmem] + [far] * 4 + [vmem] * 7 + [far],
        out_specs=[vmem] * 7,
        scratch_shapes=[pltpu.VMEM(item[0], item[1]) for item in scratch_items(spec)]
        + [
            pltpu.SemaphoreType.DMA((count_sends(sizes),)),
            pltpu.SemaphoreType.DMA((n_recv,)),
            pltpu.SemaphoreType.DMA((8,)),
        ],
        compiler_params=pltpu.CompilerParams(
            collective_id=0, has_side_effects=True, vmem_limit_bytes=60 * 1024 * 1024
        ),
        name="layer",
    )(
        tokens[0],
        segment_ids,
        bucket_table[None],
        w_qkv,
        w_out,
        w_in,
        w_down,
        gain_one[None],
        shift_one[None],
        gain_two[None],
        shift_two[None],
        bias_down[None],
        bias_in.reshape(bias_shape),
        jnp.transpose(rel_bias),
        cotangent[0],
    )
    outs = [
        ((rows, width), BF16),
        ((rows, width), BF16),
        ((w_rows, 3 * width), F32),
        ((w_rows, width), F32),
        ((w_rows, sizes.ff), F32),
        ((d_rows, width), F32),
        ((1, w_rows), F32),
        ((1, w_rows), F32),
        ((1, w_rows), F32),
        ((1, w_rows), F32),
        (bias_shape, F32),
        ((1, w_rows), F32),
        ((sizes.heads, sizes.buckets), F32),
    ]
    done = pl.pallas_call(
        functools.partial(finish_kernel, sizes),
        out_shape=[shaped(shape, kind) for shape, kind in outs],
        in_specs=[far] * 6 + [vmem],
        out_specs=[far] * 6 + [vmem] * 7,
        scratch_shapes=[pltpu.VMEM(shape, kind) for shape, kind in outs[2:6]]
        + [pltpu.VMEM(item.shape, item.dtype) for item in made[2:6] + made[0:2]]
        + [pltpu.SemaphoreType.DMA((12,))],
        compiler_params=pltpu.CompilerParams(vmem_limit_bytes=60 * 1024 * 1024),
        name="finish",
    )(*made)
    return (
        done[0][None],
        done[1][None],
        done[2],
        done[3],
        done[4],
        done[5],
        done[6][0],
        done[7][0],
        done[8][0],
        done[9][0],
        done[10].reshape(-1),
        done[11][0],
        jnp.transpose(done[12]),
    )


def solution(mesh):
    by_f, by_both = P("fsdp"), P("fsdp", "ctx", None)
    in_specs = (by_both, by_f, P()) + (by_f,) * 10 + (P(), by_both)
    out_specs = (by_both, by_both) + (by_f,) * 10 + (P(),)
    return jax.shard_map(
        functools.partial(per_device, mesh.shape["fsdp"]),
        mesh=mesh,
        in_specs=in_specs,
        out_specs=out_specs,
        check_vma=False,
    )
```

```python
import functools
import math
from types import SimpleNamespace

import jax
import jax.numpy as jnp
from jax import lax
from jax.experimental import pallas as pl
from jax.experimental.pallas import tpu as pltpu
from jax.sharding import PartitionSpec as P

MESH = pl.DeviceIdType.MESH
F32 = jnp.float32
BF16 = jnp.bfloat16
norm_eps = 1e-05
masked_low = -1e30
CTX = 4
LANES = 128


def mm(left, right, left_dim=1, right_dim=0):
    return lax.dot_general(
        left, right, (((left_dim,), (right_dim,)), ((), ())), preferred_element_type=F32
    )


def norm_stats(rows):
    centre = jnp.mean(rows, axis=-1, keepdims=True)
    centred = rows - centre
    spread = jnp.mean(centred * centred, axis=-1, keepdims=True)
    scale = lax.rsqrt(spread + norm_eps)
    return centred * scale, scale


def norm_back(d_normed, gain_row, hat, scale):
    d_hat = d_normed * gain_row
    mean_d = jnp.mean(d_hat, axis=-1, keepdims=True)
    mean_dh = jnp.mean(d_hat * hat, axis=-1, keepdims=True)
    return scale * (d_hat - mean_d - hat * mean_dh)


class Sizes:
    def __init__(self, n_f, rows, width, ff, group, buckets, heads):
        self.n_f = n_f
        self.half = n_f // 2
        self.rows = rows
        self.width = width
        self.ff = ff
        self.group = group
        self.buckets = buckets
        self.heads = heads
        self.head = width // heads
        self.w_rows = width // n_f
        self.d_rows = ff // n_f
        self.own_ff = ff // CTX
        self.part = self.d_rows // CTX
        self.owned = n_f // CTX
        self.blocks = CTX * (CTX + 1) // 2


class Links:
    def __init__(self, send_sems, recv_sems):
        self.send_sems = send_sems
        self.recv_sems = recv_sems
        self.used = 0
        self.pending = []

    def copy(self, src, dst, index, arrival, device):
        return pltpu.make_async_remote_copy(
            src_ref=src,
            dst_ref=dst,
            send_sem=self.send_sems.at[index],
            recv_sem=self.recv_sems.at[arrival],
            device_id=device,
            device_id_type=MESH,
        )

    def send(self, src, dst, arrival, device):
        self.copy(src, dst, self.used, arrival, device).start()
        self.pending.append((src, self.used, device))
        self.used += 1

    def send_all(self, pairs, arrival, devices, size):
        for (src, dst), device in zip(pairs, devices):
            self.copy(src, dst, self.used, arrival, device).start()
        self.pending.append((size, self.used, devices[0]))
        self.used += 1

    def wait(self, dst, arrival, device):
        self.copy(dst, dst, 0, arrival, device).wait_recv()

    def drain(self):
        for src, index, device in self.pending:
            self.copy(src, src, index, 0, device).wait_send()
        self.pending = []


SENDS = 96


def layer_kernel(
    sizes,
    tok_in,
    seg_in,
    table_in,
    wqkv_in,
    wout_in,
    win_in,
    wdown_in,
    vec_in0,
    vec_in1,
    vec_in2,
    vec_in3,
    vec_in4,
    bias_in_in,
    rel_in,
    dy_in,
    out_ref,
    dx_ref,
    gqk_ref,
    gv_ref,
    gout_ref,
    gin_ref,
    gdown_ref,
    small_ref,
    *scratch_refs,
):
    s, sem = name_scratch(scratch_spec(sizes), scratch_refs[:-3])
    send_sems, recv_sems, own_sems = scratch_refs[-3:]
    n_f, half, rows = sizes.n_f, sizes.half, sizes.rows
    width, w_rows, d_rows, own_ff = sizes.width, sizes.w_rows, sizes.d_rows, sizes.own_ff
    part, out_part = sizes.part, sizes.w_rows // CTX
    head = sizes.head

    c = lax.axis_index("ctx")
    f = lax.axis_index("fsdp")
    side = c // 2
    core = c % 2
    place = f // 2
    par = f % 2
    sib = side * 2 + 1 - core
    opp = (1 - side) * 2 + core
    diag = (1 - side) * 2 + 1 - core

    def ctx_dev(index):
        return {"ctx": index, "fsdp": f}

    def f_dev(index):
        return {"ctx": c, "fsdp": index}

    partner = 2 * place + 1 - par

    def other_place(step):
        return lax.rem(place + step, half)

    links = Links(send_sems, recv_sems)

    barrier = pltpu.get_barrier_semaphore()
    for step in range(1, CTX):
        pl.semaphore_signal(
            barrier, inc=1, device_id=ctx_dev(lax.rem(c + step, CTX)), device_id_type=MESH
        )
    for step in range(1, n_f):
        pl.semaphore_signal(
            barrier, inc=1, device_id=f_dev(lax.rem(f + step, n_f)), device_id_type=MESH
        )

    own_copies, leaving = [], []

    def fetch(src, dst):
        made = pltpu.make_async_copy(src, dst, own_sems.at[len(own_copies)])
        own_copies.append(made)
        made.start()
        return made

    def keep(src, dst):
        made = pltpu.make_async_copy(src, dst, own_sems.at[len(own_copies)])
        own_copies.append(made)
        made.start()
        leaving.append(made)

    first_fetches = []
    for third in range(3):
        cols = pl.ds(pl.multiple_of(third * width + c * LANES, LANES), LANES)
        first_fetches.append(
            fetch(wqkv_in.at[:, cols], s.wq.at[f, :, third * LANES : (third + 1) * LANES])
        )
    first_fetches.append(fetch(tok_in, s.tok.at[c]))
    own_block = pl.ds(pl.multiple_of(c * LANES, LANES), LANES)
    later_fetches = [
        fetch(wdown_in.at[pl.ds(pl.multiple_of(c * part, 8), part), :], s.wd.at[f]),
        fetch(wout_in.at[:, own_block], s.wo.at[c, f]),
        fetch(dy_in, s.dy.at[c]),
    ]
    small_in = (vec_in0, vec_in1, vec_in2, vec_in3, vec_in4)
    small_fetches = [fetch(ref, s.ones[at]) for at, ref in enumerate(small_in)]
    small_fetches.append(fetch(bias_in_in, s.bias))
    table_fetches = [fetch(seg_in, s.seg), fetch(table_in, s.table), fetch(rel_in, s.rel)]
    hidden_fetch = fetch(win_in, s.win)
    for made in small_fetches:
        made.wait()
    for at in range(len(small_in)):
        s.vec[f, at : at + 1, 0:w_rows] = s.ones[at][...].astype(F32)
    for at in range(s.bias.shape[0]):
        size = s.bias.shape[1]
        s.vec[f, 5:6, at * size : (at + 1) * size] = s.bias[at : at + 1, :].astype(F32)
    hidden_fetch.wait()
    for at in range(CTX):

        @pl.when(c == at)
        def pick_hidden(at=at):
            starts = [index * d_rows + at * part for index in range(n_f)]
            s.wi[f] = jnp.concatenate([s.win[:, low : low + part] for low in starts], axis=1)

    for made in first_fetches + table_fetches:
        made.wait()

    pl.semaphore_wait(barrier, CTX - 1 + n_f - 1)

    peers = [f_dev(lax.rem(f + step, n_f)) for step in range(1, n_f)]
    far = [2 * other_place(step) + par for step in range(1, half)]
    others = [ctx_dev(lax.rem(c + step, CTX)) for step in range(1, CTX)]

    def to_peers(buf, first):
        piece = buf.at[f]
        links.send_all([(piece, piece)] * (n_f - 1), first, peers, buf.at[0 : n_f - 1])

    def from_peers(buf, first):
        links.wait(buf.at[0 : n_f - 1], first, peers[0])

    def to_group(buf, first):
        piece = buf.at[c]
        links.send_all([(piece, piece)] * (CTX - 1), first, others, buf.at[0 : CTX - 1])

    def from_group(buf, first):
        links.wait(buf.at[0 : CTX - 1], first, others[0])

    def spread(buf, first):
        piece = buf.at[f]
        links.send_all(
            [(piece, piece)] * (half - 1),
            first[0] + place,
            [f_dev(to) for to in far],
            buf.at[0 : half - 1],
        )
        links.send(piece, piece, first[1], f_dev(partner))

    def pass_on(buf, first):
        pairs = []
        for step in range(1, half):
            src = far[step - 1]
            links.wait(buf.at[src], first[0] + src // 2, f_dev(src))
            links.send(buf.at[src], buf.at[src], first[1], f_dev(partner))

    def settle(buf, first):
        links.wait(buf.at[0:half], first[1], f_dev(partner))

    to_peers(s.vec, sem.vec)
    spread(s.wq, sem.wq)
    for to in (sib, opp):
        links.send(s.tok.at[c], s.tok.at[c], sem.tok + c, ctx_dev(to))
    for made in later_fetches:
        made.wait()
    own_out = s.wo.at[c]
    to_peers(own_out, sem.wo[0])
    spread(s.wi, sem.wi)
    spread(s.wd, sem.wd)

    ids = lax.broadcasted_iota(jnp.int32, (sizes.buckets, sizes.group), 0)
    onehot = (ids == s.table[...]).astype(BF16)
    s.hot[...] = onehot.astype(F32)
    s.bvec[...] = mm(s.rel[...], onehot)
    for h in range(2):
        row = s.bvec[pl.ds(2 * c + h, 1), :]
        for delta in range(CTX):
            now = row[:, delta * rows : (delta + 1) * rows]
            before = row[:, (delta - 1) * rows : delta * rows] if delta else now
            wide = jnp.broadcast_to(jnp.concatenate([now, before], axis=1), (rows, 2 * rows))
            turned = pltpu.roll(wide, 0, 1, stride=1, stride_axis=0)
            s.tile[h, delta] = turned[:, :rows]
    seg_f = s.seg[...].astype(F32)
    for at in range(CTX):
        piece = jnp.broadcast_to(seg_f[:, at * rows : (at + 1) * rows], (rows, rows))
        s.segk[at] = jnp.transpose(piece)
    key_pos = lax.broadcasted_iota(jnp.int32, (rows, rows), 0)
    query_pos = lax.broadcasted_iota(jnp.int32, (rows, rows), 1)
    for q_at in range(CTX):
        seg_q = jnp.broadcast_to(seg_f[:, q_at * rows : (q_at + 1) * rows], (rows, rows))
        for k_at in range(q_at + 1):
            seg_k = s.segk[k_at]
            allowed = (seg_k == 0.0) | (seg_k == seg_q)
            if q_at == k_at:
                allowed = allowed & (key_pos <= query_pos)
            for h in range(2):
                block = q_at * (q_at + 1) // 2 + k_at
                s.bm[h, block] = jnp.where(allowed, s.tile[h, q_at - k_at], masked_low)

    from_peers(s.vec, sem.vec)

    def joined(pieces, count, size):
        total = count * size
        spot = lax.broadcasted_iota(jnp.int32, (size, total), 1) % size
        which = lax.broadcasted_iota(jnp.int32, (size, total), 0)
        spreader = (spot == which).astype(BF16)
        flat = mm(pieces.astype(BF16), spreader)
        owner = lax.broadcasted_iota(jnp.int32, (count, total), 1) // size
        mine = owner == lax.broadcasted_iota(jnp.int32, (count, total), 0)
        return jnp.sum(jnp.where(mine, flat, 0.0), axis=0, keepdims=True)

    for at in range(5):
        s.vrow[at : at + 1, :] = joined(s.vec[:, at, 0:w_rows], n_f, w_rows)
    for at in range(CTX):

        @pl.when(c == at)
        def pick_bias(at=at):
            s.vrow[5:6, :] = joined(s.vec[:, 5, at * part : (at + 1) * part], n_f, part)

    gain_one, shift_one = s.vrow[0:1, :], s.vrow[1:2, :]
    gain_two, shift_two = s.vrow[2:3, :], s.vrow[3:4, :]
    bias_down_row, bias_in_row = s.vrow[4:5, :], s.vrow[5:6, :]

    step_rows = 64

    def row_loop(body, count=rows):
        def run(at, carried):
            body(pl.ds(pl.multiple_of(at * step_rows, step_rows), step_rows))
            return carried

        lax.fori_loop(0, count // step_rows, run, 0)

    def first_norm(chunk):
        def body(part):
            hat, scale = norm_stats(s.tok[chunk, part, :].astype(F32))
            s.fn[chunk, part, :] = (hat * gain_one + shift_one).astype(BF16)

        row_loop(body)

    def whole(buf, count, size, kept):
        if size % 16 == 0:
            return buf[...].reshape(count * size, buf.shape[2])
        for at in range(count):
            kept[at * size : (at + 1) * size, :] = buf[at]
        return kept[...]

    head_rows = lax.broadcasted_iota(jnp.int32, (LANES, rows), 0) // head

    def project(chunk):
        weights = whole(s.wq, n_f, w_rows, s.flat_wq)
        made = mm(s.fn[chunk], weights)
        queries = made[:, 0:LANES].astype(BF16).astype(F32) * (head ** -0.5)
        keys = made[:, LANES : 2 * LANES]
        values = made[:, 2 * LANES : 3 * LANES]
        s.k[chunk] = keys.astype(BF16)
        s.v[chunk] = values.astype(BF16)
        s.kt[chunk] = jnp.transpose(keys).astype(BF16)
        s.vt[chunk] = jnp.transpose(values).astype(BF16)
        turned = jnp.transpose(queries)
        for h in range(2):
            kept = jnp.where(head_rows == h, turned, 0.0)
            s.qt[h, chunk] = kept.astype(BF16)
            s.q[h, chunk] = jnp.transpose(kept).astype(BF16)

    first_norm(c)
    pass_on(s.wq, sem.wq)
    links.wait(s.tok.at[sib], sem.tok + sib, ctx_dev(sib))
    first_norm(sib)
    links.wait(s.tok.at[opp], sem.tok + opp, ctx_dev(opp))
    links.send(s.tok.at[opp], s.tok.at[opp], sem.tok + opp, ctx_dev(sib))
    first_norm(opp)

    for to in (sib, opp):
        links.send(s.dy.at[c], s.dy.at[c], sem.dy + c, ctx_dev(to))

    def share_out(to, block):
        links.send(s.wo.at[block], s.wo.at[block], sem.wo[1] + block, ctx_dev(to))

    def wait_out(block, via):
        links.wait(s.wo.at[block], sem.wo[1] + block, ctx_dev(via))

    settle(s.wq, sem.wq)
    project(c)
    project(sib)
    project(opp)
    links.wait(s.tok.at[diag], sem.tok + diag, ctx_dev(sib))
    first_norm(diag)
    project(diag)
    from_peers(own_out, sem.wo[0])
    share_out(sib, c)
    share_out(opp, c)

    def attend(chunk):
        first_block = chunk * (chunk + 1) // 2

        def score_pass(k_at, tops):
            keys = s.k[k_at]
            grown = []
            for h in range(2):
                scores = mm(keys, s.qt[h, chunk]) + s.bm[h, first_block + k_at]
                s.sc[h, k_at] = scores
                grown.append(jnp.maximum(tops[h], jnp.max(scores, axis=0, keepdims=True)))
            return tuple(grown)

        low = jnp.full((1, rows), masked_low, F32)
        tops = lax.fori_loop(0, chunk + 1, score_pass, (low, low))
        s.acc[...] = jnp.zeros((LANES, rows), F32)

        def value_pass(k_at, sums):
            grown = []
            for h in range(2):
                weights = jnp.exp(s.sc[h, k_at] - tops[h])
                grown.append(sums[h] + jnp.sum(weights, axis=0, keepdims=True))
                rounded = weights.astype(BF16)
                s.e[h, first_block + k_at] = rounded
                part = slice(h * head, (h + 1) * head)
                s.acc[part, :] += mm(s.vt[k_at, part, :], rounded)
            return tuple(grown)

        none = jnp.zeros((1, rows), F32)
        sums = lax.fori_loop(0, chunk + 1, value_pass, (none, none))
        for h in range(2):
            part = slice(h * head, (h + 1) * head)
            inverse = 1.0 / sums[h]
            s.linv[chunk, h : h + 1, :] = inverse
            s.att_t[chunk, part, :] = s.acc[part, :] * inverse
        s.att[c, chunk] = jnp.transpose(s.att_t[chunk]).astype(BF16)

    def att_slot(owner, chunk):
        return owner * CTX + chunk

    def send_att(chunk):
        piece = s.att.at[c, chunk]
        for to in (sib, opp):
            links.send(piece, piece, sem.att + att_slot(c, chunk), ctx_dev(to))

    def wait_att(owner, chunk, via):
        links.wait(s.att.at[owner, chunk], sem.att + att_slot(owner, chunk), ctx_dev(via))

    def pass_att(chunk):
        wait_att(opp, chunk, opp)
        piece = s.att.at[opp, chunk]
        links.send(piece, piece, sem.att + att_slot(opp, chunk), ctx_dev(sib))

    mine = [lax.rem(2 * side + step, CTX) for step in range(CTX)]
    theirs = [lax.rem(2 * (1 - side) + step, CTX) for step in range(CTX)]
    attend(mine[0])
    send_att(mine[0])
    attend(mine[1])
    send_att(mine[1])
    pass_on(s.wi, sem.wi)
    pass_att(theirs[0])
    wait_out(opp, opp)
    share_out(sib, opp)
    attend(mine[2])
    send_att(mine[2])
    pass_att(theirs[1])
    links.wait(s.dy.at[opp], sem.dy + opp, ctx_dev(opp))
    links.send(s.dy.at[opp], s.dy.at[opp], sem.dy + opp, ctx_dev(sib))
    attend(mine[3])
    send_att(mine[3])
    pass_on(s.wd, sem.wd)

    wait_out(sib, sib)
    wait_out(diag, sib)
    for block in range(CTX):
        cols = slice(block * LANES, (block + 1) * LANES)
        if w_rows % 16 == 0:
            s.wo_flat[:, cols] = s.wo[block].reshape(width, LANES)
        else:
            for at in range(n_f):
                s.wo_flat[at * w_rows : (at + 1) * w_rows, cols] = s.wo[block, at]

    def gather_att(chunk):
        wait_att(sib, chunk, sib)
        wait_att(diag, chunk, sib)

    def feed(chunk):
        gather_att(chunk)
        mixed = jnp.zeros((rows, width), F32)
        for owner in range(CTX):
            mixed += mm(
                s.att[owner, chunk], s.wo_flat[owner * LANES : (owner + 1) * LANES, :]
            )
        s.mid[...] = mixed + s.tok[chunk].astype(F32)

        def normed(rng):
            hat, scale = norm_stats(s.mid[rng, :])
            s.sn[chunk, rng, :] = (hat * gain_two + shift_two).astype(BF16)

        row_loop(normed)
        s.inner[chunk] = mm(s.sn[chunk], whole(s.wi, n_f, w_rows, s.flat_wi))

    def feed_back(chunk):
        w_down = whole(s.wd, n_f, part, s.flat_wd)
        s.dact[...] = mm(s.dy[chunk], w_down, 1, 1)

        def gelu(rng):
            inner = s.inner[chunk, rng, :] + bias_in_row
            phi = 0.5 + 0.5 * lax.erf(inner * (2.0 ** -0.5))
            slope = phi + inner * (jnp.exp(-0.5 * inner * inner) * (1.0 / math.sqrt(2.0 * math.pi)))
            s.actv[chunk, rng, :] = (inner * phi).astype(BF16)
            s.din[chunk, rng, :] = (s.dact[rng, :] * slope).astype(BF16)

        row_loop(gelu)
        return mm(s.din[chunk], whole(s.wi, n_f, w_rows, s.flat_wi), 1, 1)

    def scatter_first(group, first, part):
        group[0][...] = part.astype(BF16)
        links.send(group[0], group[1], first[0], ctx_dev(sib))

    def scatter_second(group, first, part):
        links.wait(group[1], first[0], ctx_dev(sib))
        group[2][...] = (part + group[1][...].astype(F32)).astype(BF16)
        links.send(group[2], group[3], first[1], ctx_dev(opp))

    def scatter_third(group, first, part):
        group[4][...] = part.astype(BF16)
        links.send(group[4], group[5], first[2], ctx_dev(sib))

    def scatter_wait(group, first):
        links.wait(group[5], first[2], ctx_dev(sib))
        links.wait(group[3], first[1], ctx_dev(opp))

    def scatter_sum(group, part):
        return group[3][part, :].astype(F32) + group[5][part, :].astype(F32)

    settle(s.wi, sem.wi)
    feed(diag)
    pass_att(theirs[2])
    feed(opp)
    pass_att(theirs[3])
    feed(sib)
    feed(c)
    settle(s.wd, sem.wd)
    links.wait(s.dy.at[diag], sem.dy + diag, ctx_dev(sib))
    scatter_first(s.rs_s, sem.rs_s, feed_back(diag))
    scatter_second(s.rs_s, sem.rs_s, feed_back(opp))
    links.wait(s.dy.at[sib], sem.dy + sib, ctx_dev(sib))
    scatter_third(s.rs_s, sem.rs_s, feed_back(sib))
    s.dsec[...] = feed_back(c)

    def even_pieces(group, left, right, cols, size):
        for at in range(left.shape[2] // LANES):
            lhs = left[:, :, at * LANES : (at + 1) * LANES].reshape(CTX * rows, LANES)
            made = mm(lhs, right[...].reshape(CTX * rows, cols), 0, 0).astype(BF16)
            for piece in range(LANES // size):
                to = at * (LANES // size) + piece
                group[0][to % 2, to // 2] = made[piece * size : (piece + 1) * size, :]

    def grad_pair(group, first):
        links.send(group[0].at[1 - par], group[1], first[0], f_dev(partner))

    def grad_even_second(group, first):
        links.wait(group[1], first[0], f_dev(partner))
        group[2][...] = (
            group[0][par].astype(F32) + group[1][...].astype(F32)
        ).astype(BF16)
        pairs = [(group[2].at[to // 2], group[3].at[place]) for to in far]
        links.send_all(pairs, first[1], [f_dev(to) for to in far], group[3].at[0 : half - 1])

    def grad_even_third(group, first):
        links.wait(group[3].at[0 : half - 1], first[1], f_dev(far[0]))
        total = group[2][place].astype(F32)
        for src in far:
            total += group[3][src // 2].astype(F32)
        group[4][c] = total.astype(BF16)
        to_group(group[4], first[2])

    def grad_direct(group, first):
        pairs = [
            (group[0].at[lax.rem(f + step, n_f)], group[1].at[f]) for step in range(1, n_f)
        ]
        links.send_all(pairs, first[0], peers, group[1].at[0 : n_f - 1])

    def grad_direct_sum(group, first):
        from_peers(group[1], first[0])
        total = group[0][f].astype(F32)
        for step in range(1, n_f):
            total += group[1][lax.rem(f + step, n_f)].astype(F32)
        group[2][c] = total.astype(BF16)
        to_group(group[2], first[1])

    even_pieces(s.gd, s.actv, s.dy, width, part)
    grad_pair(s.gd, sem.gd)
    even_pieces(s.gi, s.sn, s.din, own_ff, w_rows)
    grad_pair(s.gi, sem.gi)
    w_down = whole(s.wd, n_f, part, s.flat_wd)
    scatter_first(s.rs_o, sem.rs_o, mm(s.actv[diag], w_down))
    scatter_third(s.rs_o, sem.rs_o, mm(s.actv[sib], w_down))

    scatter_wait(s.rs_s, sem.rs_s)
    s.vg[...] = jnp.zeros_like(s.vg)

    def second_back(rng):
        hat, scale = norm_stats(s.mid[rng, :])
        d_second = s.dsec[rng, :] + scatter_sum(s.rs_s, rng)
        d_result = s.dy[c, rng, :].astype(F32)
        d_middle = d_result + norm_back(d_second, gain_two, hat, scale)
        s.dmid[rng, :] = d_middle
        s.dmx[rng, :] = d_middle.astype(BF16)
        s.vg[2:3, :] += jnp.sum(d_second * hat, axis=0, keepdims=True)
        s.vg[3:4, :] += jnp.sum(d_second, axis=0, keepdims=True)
        s.vg[4:5, :] += jnp.sum(d_result, axis=0, keepdims=True)

    row_loop(second_back)
    d_att = mm(s.wo_flat[...], s.dmx[...], 1, 1)
    s.dat_out[...] = d_att.astype(BF16).reshape(CTX, LANES, rows)
    for to in (opp, diag, sib):
        links.send(s.dat_out.at[to], s.dat.at[c], sem.dat + c, ctx_dev(to))
    s.dat[c] = s.dat_out[c]
    for owner in range(CTX):
        made = mm(s.att[owner, c], s.dmx[...], 0, 0).astype(BF16)
        for piece in range(LANES // w_rows):
            at = owner * (LANES // w_rows) + piece
            for part_at in range(CTX):
                low = piece * w_rows + part_at * out_part
                s.go_own[part_at % 2, part_at // 2, at] = made[low : low + out_part, :]
    links.send(s.go_own.at[1 - core], s.go_core, sem.go_core, ctx_dev(sib))
    grad_even_second(s.gd, sem.gd)
    links.wait(s.go_core, sem.go_core, ctx_dev(sib))
    s.go_two[...] = (
        s.go_own[core].astype(F32) + s.go_core[...].astype(F32)
    ).astype(BF16)
    links.send(s.go_two.at[1 - side], s.go_side, sem.go_side, ctx_dev(opp))
    scatter_second(s.rs_o, sem.rs_o, mm(s.actv[opp], w_down))
    s.outp[...] = s.mid[...] + mm(s.actv[c], w_down) + bias_down_row
    for at in range(CTX):

        def bias_rows(rng, at=at):
            s.vg[5:6, :] += jnp.sum(s.din[at, rng, :].astype(F32), axis=0, keepdims=True)

        row_loop(bias_rows)

    for src in (sib, opp, diag):
        links.wait(s.dat.at[src], sem.dat + src, ctx_dev(src))
    for at in range(CTX):
        got = s.dat[at].astype(F32)
        for h in range(2):
            part = slice(h * head, (h + 1) * head)
            scaled = (got * s.linv[at, h : h + 1, :]).astype(BF16)
            kept = jnp.where(head_rows == h, scaled.astype(F32), 0.0)
            s.dat_t[h, at] = kept.astype(BF16)
            s.dat_n[h, at] = jnp.transpose(kept).astype(BF16)
            s.delta[at, h : h + 1, :] = jnp.sum(
                kept[part, :] * s.att_t[at, part, :], axis=0, keepdims=True
            )
        s.dqt[at] = jnp.zeros((LANES, rows), F32)
        s.dk[at] = jnp.zeros((rows, LANES), F32)
    s.dbm[...] = jnp.zeros_like(s.dbm)

    def block_pair(q_at, k_at):
        block = q_at * (q_at + 1) // 2 + k_at
        values = s.v[k_at]
        for h in range(2):
            lanes = slice(h * head, (h + 1) * head)
            d_probs = mm(values, s.dat_t[h, q_at])
            rounded = s.e[h, block]
            d_scores = rounded.astype(F32) * (d_probs - s.delta[q_at, h : h + 1, :])
            s.dbm[h, q_at - k_at] += d_scores
            low = d_scores.astype(BF16)
            s.dk[k_at] += mm(low, s.q[h, q_at])
            s.dqt[q_at, lanes, :] += mm(s.kt[k_at, lanes, :], low)

    def query_row(upper):
        def run(lower, carried):
            shift = side * (CTX - 1 - upper - lower)
            block_pair(upper + shift, lower + shift)
            return carried

        lax.fori_loop(0, upper + 1, run, 0)

    def pack(chunk):
        s.dp[chunk, :, 0:LANES] = (jnp.transpose(s.dqt[chunk]) * (head ** -0.5)).astype(BF16)
        s.dp[chunk, :, LANES : 2 * LANES] = s.dk[chunk].astype(BF16)

    w_qkv = whole(s.wq, n_f, w_rows, s.flat_wq)

    def back_first(chunk):
        s.dsec[...] = mm(s.dp[chunk], w_qkv, 1, 1)

        def add_rows(rng):
            part_rows = s.dsec[rng, :]
            s.vg[0:1, :] += jnp.sum(s.fn[chunk, rng, :].astype(F32) * part_rows, axis=0, keepdims=True)
            s.vg[1:2, :] += jnp.sum(part_rows, axis=0, keepdims=True)

        return add_rows

    def value_grads(k_at):
        made = jnp.zeros((rows, LANES), F32)
        for q_at in range(k_at, CTX):
            block = q_at * (q_at + 1) // 2 + k_at
            for h in range(2):
                made += mm(s.e[h, block], s.dat_n[h, q_at])
        s.dp[k_at, :, 2 * LANES : 3 * LANES] = made.astype(BF16)

    def qkv_pieces(group, cols):
        for at in range(width // LANES):
            lhs = s.fn[:, :, at * LANES : (at + 1) * LANES].reshape(CTX * rows, LANES)
            rhs = s.dp[:, :, cols].reshape(CTX * rows, cols.stop - cols.start)
            made = mm(lhs, rhs, 0, 0).astype(BF16)
            for piece in range(LANES // w_rows):
                to = at * (LANES // w_rows) + piece
                group[0][to] = made[piece * w_rows : (piece + 1) * w_rows, :]

    for at in range(CTX):
        value_grads(at)
    qkv_pieces(s.gv, slice(2 * LANES, 3 * LANES))
    grad_direct(s.gv, sem.gv)
    query_row(3)
    grad_even_second(s.gi, sem.gi)
    links.wait(s.go_side, sem.go_side, ctx_dev(opp))
    s.go[0][...] = (s.go_two[side].astype(F32) + s.go_side[...].astype(F32)).astype(BF16)
    grad_direct(s.go, sem.go)
    query_row(2)
    pack(diag)
    pack(opp)
    sums = back_first(diag)
    scatter_first(s.rs_f, sem.rs_f, s.dsec[...])
    row_loop(sums)
    sums = back_first(opp)
    scatter_second(s.rs_f, sem.rs_f, s.dsec[...])
    row_loop(sums)
    query_row(1)
    query_row(0)
    pack(sib)
    pack(c)
    qkv_pieces(s.gq, slice(0, 2 * LANES))
    grad_direct(s.gq, sem.gq)
    grad_direct_sum(s.gv, sem.gv)
    sums = back_first(sib)
    scatter_third(s.rs_f, sem.rs_f, s.dsec[...])
    row_loop(sums)
    sums = back_first(c)
    row_loop(sums)

    for h in range(2):
        pieces = []
        for delta in range(CTX):
            block = s.dbm[h, delta]
            wide = jnp.concatenate([block, jnp.zeros((rows, rows), F32)], axis=1)
            count = rows
            while count > 1:
                count //= 2
                turned = pltpu.roll(wide[count : 2 * count, :], 2 * rows - count, 1)
                wide = wide[0:count, :] + turned
            pieces.append(wide)
        total = []
        for delta in range(CTX):
            here = pieces[delta][:, 0:rows]
            if delta + 1 < CTX:
                here = here + pieces[delta + 1][:, rows : 2 * rows]
            total.append(here)
        dist = jnp.concatenate(total, axis=1)
        bucket_sums = lax.dot_general(
            jnp.broadcast_to(dist, (8, sizes.group)),
            s.hot[...],
            (((1,), (1,)), ((), ())),
            preferred_element_type=F32,
            precision=lax.Precision.HIGHEST,
        )
        s.vg[6 + h : 7 + h, 0 : sizes.buckets] = bucket_sums[0:1, :]

    s.vg[0:1, :] = (s.vg[0:1, :] - shift_one * s.vg[1:2, :]) / gain_one
    for to in range(n_f):
        s.vgp[to, :, 0:w_rows] = s.vg[:, to * w_rows : (to + 1) * w_rows]
        s.vgp[to, 6:8, 0 : sizes.buckets] = s.vg[6:8, 0 : sizes.buckets]
    pairs = [(s.vgp.at[lax.rem(f + step, n_f)], s.vgf.at[f]) for step in range(1, n_f)]
    links.send_all(pairs, sem.vgf, peers, s.vgf.at[0 : n_f - 1])

    grad_even_third(s.gd, sem.gd)
    scatter_wait(s.rs_f, sem.rs_f)

    def first_back(rng):
        hat, scale = norm_stats(s.tok[c, rng, :].astype(F32))
        d_first = s.dsec[rng, :] + scatter_sum(s.rs_f, rng)
        d_x = s.dmid[rng, :] + norm_back(d_first, gain_one, hat, scale)
        s.dx[rng, :] = d_x.astype(BF16)

    row_loop(first_back)
    keep(s.dx, dx_ref)
    grad_direct_sum(s.gq, sem.gq)
    from_peers(s.vgf, sem.vgf)
    total = s.vgp[f]
    for step in range(1, n_f):
        total += s.vgf[lax.rem(f + step, n_f)]
    s.vgc[c] = total
    to_group(s.vgc, sem.vgc)
    grad_direct_sum(s.go, sem.go)
    grad_even_third(s.gi, sem.gi)

    scatter_wait(s.rs_o, sem.rs_o)
    s.out[...] = (
        s.outp[...] + s.rs_o[3][...].astype(F32) + s.rs_o[5][...].astype(F32)
    ).astype(BF16)
    keep(s.out, out_ref)
    from_group(s.gd[4], sem.gd[2])
    keep(s.gd[4], gdown_ref)
    from_group(s.gv[2], sem.gv[1])
    keep(s.gv[2], gv_ref)
    from_group(s.gq[2], sem.gq[1])
    keep(s.gq[2], gqk_ref)
    from_group(s.vgc, sem.vgc)
    keep(s.vgc, small_ref)
    from_group(s.go[2], sem.go[1])
    keep(s.go[2], gout_ref)
    from_group(s.gi[4], sem.gi[2])
    keep(s.gi[4], gin_ref)
    links.drain()
    for made in leaving:
        made.wait()


def finish_kernel(
    sizes,
    out_in,
    dx_in,
    gqk_in,
    gv_in,
    gout_in,
    gin_in,
    gdown_in,
    small_in,
    out_ref,
    dx_ref,
    gqkv_ref,
    gout_ref,
    gin_ref,
    gdown_ref,
    gg1_ref,
    gs1_ref,
    gg2_ref,
    gs2_ref,
    gbi_ref,
    gbd_ref,
    grel_ref,
    gqkv,
    gout,
    gin,
    gdown,
    gqk_low,
    gv_low,
    gout_low,
    gin_low,
    gdown_low,
    out_low,
    dx_low,
    sems,
):
    made = []

    def start(src, dst):
        copy = pltpu.make_async_copy(src, dst, sems.at[len(made)])
        copy.start()
        made.append(copy)
        return copy

    loads = [
        start(gdown_in, gdown_low),
        start(gin_in, gin_low),
        start(gqk_in, gqk_low),
        start(gout_in, gout_low),
    ]
    loads += [start(out_in, out_low), start(dx_in, dx_low), start(gv_in, gv_low)]
    width, own_ff = sizes.width, sizes.own_ff
    loads[0].wait()
    for at in range(CTX):
        gdown[at * sizes.part : (at + 1) * sizes.part, :] = gdown_low[at].astype(F32)
    stores = [start(gdown, gdown_ref)]
    loads[1].wait()
    part = sizes.part
    for index in range(sizes.n_f):
        lanes = slice(index * part, (index + 1) * part)
        joined = jnp.concatenate([gin_low[at, :, lanes].astype(F32) for at in range(CTX)], axis=1)
        gin[:, index * CTX * part : (index + 1) * CTX * part] = joined
    stores.append(start(gin, gin_ref))
    loads[2].wait()
    loads[6].wait()
    for at in range(CTX):
        for third in range(3):
            low = third * width + at * LANES
            if third == 2:
                got = gv_low[at]
            else:
                got = gqk_low[at, :, third * LANES : (third + 1) * LANES]
            gqkv[:, low : low + LANES] = got.astype(F32)
    stores.append(start(gqkv, gqkv_ref))
    loads[3].wait()
    out_part = sizes.w_rows // CTX
    for at in range(CTX):
        gout[at * out_part : (at + 1) * out_part, :] = gout_low[at].astype(F32)
    stores.append(start(gout, gout_ref))
    loads[4].wait()
    stores.append(start(out_low, out_ref))
    loads[5].wait()
    stores.append(start(dx_low, dx_ref))
    total = jnp.sum(small_in[...], axis=0)
    for at, ref in enumerate((gg1_ref, gs1_ref, gg2_ref, gs2_ref, gbd_ref)):
        ref[...] = total[at : at + 1, 0 : sizes.w_rows]
    size = gbi_ref.shape[1]
    hidden = jnp.concatenate([small_in[at, 5:6, 0 : sizes.part] for at in range(CTX)], axis=1)
    for at in range(gbi_ref.shape[0]):
        gbi_ref[at : at + 1, :] = hidden[:, at * size : (at + 1) * size]
    for at in range(CTX):
        grel_ref[2 * at : 2 * at + 2, :] = small_in[at, 6:8, 0 : sizes.buckets]
    for copy in stores:
        copy.wait()


def scratch_spec(z):
    rows, width, group = z.rows, z.width, z.group
    blocks = CTX * (CTX + 1) // 2
    act = (CTX, rows, width)
    hidden = (CTX, rows, z.own_ff)
    tall = (CTX, rows, LANES)
    wide = (CTX, LANES, rows)
    squares = (2, CTX, rows, rows)

    def scatter():
        flat = ((rows, width), BF16)
        landing = ((rows, width), BF16, 1)
        return [flat, landing, flat, landing, flat, landing]

    def even(size, cols):
        part = (z.half, size, cols)
        return [
            ((2,) + part, BF16),
            (part, BF16, 1),
            (part, BF16),
            (part, BF16, 1),
            ((CTX, size, cols), BF16, 1),
        ]

    def direct(size, cols):
        whole = (z.n_f, size, cols)
        return [(whole, BF16), (whole, BF16, 1), ((CTX, size, cols), BF16, 1)]

    out_part = z.w_rows // CTX
    out_rows = (z.n_f, out_part, width)
    spec = dict(
        tok=(act, BF16, CTX),
        dy=(act, BF16, CTX),
        fn=(act, BF16),
        wq=((z.n_f, z.w_rows, 3 * LANES), BF16, z.half, 1),
        wo=((CTX, z.n_f, z.w_rows, LANES), BF16, 1, CTX),
        wo_flat=((width, width), BF16),
        wi=((z.n_f, z.w_rows, z.own_ff), BF16, z.half, 1),
        wd=((z.n_f, z.part, width), BF16, z.half, 1),
        vec=((z.n_f, 8, max(z.d_rows, LANES)), F32, 1),
        ones=[((1, z.w_rows), BF16)] * 5,
        bias=((max(1, z.d_rows // LANES), min(LANES, z.d_rows)), BF16),
        seg=((1, group), jnp.int32),
        table=((1, group), jnp.int32),
        rel=((z.heads, z.buckets), BF16),
        win=((z.w_rows, z.ff), BF16),
        out=((rows, width), BF16),
        dx=((rows, width), BF16),
        vrow=((8, width), F32),
        hot=((z.buckets, group), F32),
        bvec=((8, group), F32),
        tile=(squares, F32),
        segk=((CTX, rows, rows), F32),
        bm=((2, blocks, rows, rows), F32),
        k=(tall, BF16),
        v=(tall, BF16),
        kt=(wide, BF16),
        vt=(wide, BF16),
        qt=((2,) + wide, BF16),
        q=((2,) + tall, BF16),
        sc=(squares, F32),
        e=((2, blocks, rows, rows), BF16),
        acc=((LANES, rows), F32),
        linv=((CTX, 8, rows), F32),
        att_t=(wide, F32),
        att=((CTX,) + tall, BF16, CTX * CTX),
        mid=((rows, width), F32),
        sn=(act, BF16),
        inner=((CTX, rows, z.own_ff), F32),
        dact=((rows, z.own_ff), F32),
        actv=(hidden, BF16),
        din=(hidden, BF16),
        dsec=((rows, width), F32),
        outp=((rows, width), F32),
        dmid=((rows, width), F32),
        dmx=((rows, width), BF16),
        dat_out=(wide, BF16),
        dat=(wide, BF16, CTX),
        dat_t=((2,) + wide, BF16),
        dat_n=((2,) + tall, BF16),
        delta=((CTX, 8, rows), F32),
        dqt=(wide, F32),
        dbm=(squares, F32),
        dk=(tall, F32),
        dp=((CTX, rows, 3 * LANES), BF16),
        vg=((8, width), F32),
        vgp=((z.n_f, 8, LANES), F32),
        vgf=((z.n_f, 8, LANES), F32, 1),
        vgc=((CTX, 8, LANES), F32, 1),
        rs_s=scatter(),
        rs_o=scatter(),
        rs_f=scatter(),
        gq=direct(z.w_rows, 2 * LANES),
        gv=direct(z.w_rows, LANES),
        gi=even(z.w_rows, z.own_ff),
        gd=even(z.part, width),
        go=direct(out_part, width),
        go_own=((2, 2) + out_rows, BF16),
        go_core=((2,) + out_rows, BF16, 1),
        go_two=((2,) + out_rows, BF16),
        go_side=(out_rows, BF16, 1),
    )
    if z.w_rows % 16:
        spec.update(
            flat_wq=((width, 3 * LANES), BF16),
            flat_wi=((width, z.own_ff), BF16),
        )
    else:
        spec.update(flat_wq=((8, LANES), BF16), flat_wi=((8, LANES), BF16))
    flat_shape = (z.own_ff, width) if z.part % 16 else (8, LANES)
    spec.update(flat_wd=(flat_shape, BF16))
    return spec


def scratch_items(spec):
    for item in spec.values():
        if isinstance(item, list):
            yield from item
        else:
            yield item


def name_scratch(spec, refs):
    refs = iter(refs)
    by_name, first, used = {}, {}, 0
    for name, item in spec.items():
        entries = item if isinstance(item, list) else [item]
        held, starts = [], []
        for entry in entries:
            held.append(next(refs))
            for count in entry[2:]:
                starts.append(used)
                used += count
        by_name[name] = held if isinstance(item, list) else held[0]
        if starts:
            first[name] = starts if isinstance(item, list) or len(starts) > 1 else starts[0]
    return SimpleNamespace(**by_name), SimpleNamespace(**first)


def per_device(
    n_f,
    tokens,
    segment_ids,
    bucket_table,
    w_qkv,
    w_out,
    w_in,
    w_down,
    gain_one,
    shift_one,
    gain_two,
    shift_two,
    bias_in,
    bias_down,
    rel_bias,
    cotangent,
):
    sizes = Sizes(
        n_f,
        tokens.shape[1],
        tokens.shape[2],
        w_in.shape[1],
        segment_ids.shape[1],
        rel_bias.shape[0],
        rel_bias.shape[1],
    )
    rows, width, w_rows, d_rows = sizes.rows, sizes.width, sizes.w_rows, sizes.d_rows
    vmem = pl.BlockSpec(memory_space=pltpu.VMEM)
    far = pl.BlockSpec(memory_space=pltpu.HBM)
    spec = scratch_spec(sizes)
    n_recv = sum(sum(item[2:]) for item in scratch_items(spec))
    bias_shape = (max(1, d_rows // LANES), min(LANES, d_rows))
    shaped = jax.ShapeDtypeStruct
    made = pl.pallas_call(
        functools.partial(layer_kernel, sizes),
        out_shape=[
            shaped((rows, width), BF16),
            shaped((rows, width), BF16),
            shaped((CTX, w_rows, 2 * LANES), BF16),
            shaped((CTX, w_rows, LANES), BF16),
            shaped((CTX, w_rows // CTX, width), BF16),
            shaped((CTX, w_rows, sizes.own_ff), BF16),
            shaped((CTX, sizes.part, width), BF16),
            shaped((CTX, 8, LANES), F32),
        ],
        in_specs=[far] * 15,
        out_specs=[far] * 8,
        scratch_shapes=[pltpu.VMEM(item[0], item[1]) for item in scratch_items(spec)]
        + [
            pltpu.SemaphoreType.DMA((SENDS,)),
            pltpu.SemaphoreType.DMA((n_recv,)),
            pltpu.SemaphoreType.DMA((26,)),
        ],
        compiler_params=pltpu.CompilerParams(
            collective_id=0, has_side_effects=True, vmem_limit_bytes=60 * 1024 * 1024
        ),
        name="layer",
    )(
        tokens[0],
        segment_ids,
        bucket_table[None],
        w_qkv,
        w_out,
        w_in,
        w_down,
        gain_one[None],
        shift_one[None],
        gain_two[None],
        shift_two[None],
        bias_down[None],
        bias_in.reshape(bias_shape),
        jnp.transpose(rel_bias),
        cotangent[0],
    )
    outs = [
        ((rows, width), BF16),
        ((rows, width), BF16),
        ((w_rows, 3 * width), F32),
        ((w_rows, width), F32),
        ((w_rows, sizes.ff), F32),
        ((d_rows, width), F32),
        ((1, w_rows), F32),
        ((1, w_rows), F32),
        ((1, w_rows), F32),
        ((1, w_rows), F32),
        (bias_shape, F32),
        ((1, w_rows), F32),
        ((sizes.heads, sizes.buckets), F32),
    ]
    done = pl.pallas_call(
        functools.partial(finish_kernel, sizes),
        out_shape=[shaped(shape, kind) for shape, kind in outs],
        in_specs=[far] * 7 + [vmem],
        out_specs=[far] * 6 + [vmem] * 7,
        scratch_shapes=[pltpu.VMEM(shape, kind) for shape, kind in outs[2:6]]
        + [pltpu.VMEM(item.shape, item.dtype) for item in made[2:7] + made[0:2]]
        + [pltpu.SemaphoreType.DMA((14,))],
        compiler_params=pltpu.CompilerParams(vmem_limit_bytes=60 * 1024 * 1024),
        name="finish",
    )(*made)
    return (
        done[0][None],
        done[1][None],
        done[2],
        done[3],
        done[4],
        done[5],
        done[6][0],
        done[7][0],
        done[8][0],
        done[9][0],
        done[10].reshape(-1),
        done[11][0],
        jnp.transpose(done[12]),
    )


def solution(mesh):
    by_f, by_both = P("fsdp"), P("fsdp", "ctx", None)
    in_specs = (by_both, by_f, P()) + (by_f,) * 10 + (P(), by_both)
    out_specs = (by_both, by_both) + (by_f,) * 10 + (P(),)
    return jax.shard_map(
        functools.partial(per_device, mesh.shape["fsdp"]),
        mesh=mesh,
        in_specs=in_specs,
        out_specs=out_specs,
        check_vma=False,
    )
```

```python
import functools
import math
from types import SimpleNamespace

import jax
import jax.numpy as jnp
from jax import lax
from jax.experimental import pallas as pl
from jax.experimental.pallas import tpu as pltpu
from jax.sharding import PartitionSpec as P

MESH = pl.DeviceIdType.MESH
F32 = jnp.float32
BF16 = jnp.bfloat16
norm_eps = 1e-05
masked_low = -1e30
CTX = 4
LANES = 128


def mm(left, right, left_dim=1, right_dim=0):
    return lax.dot_general(
        left, right, (((left_dim,), (right_dim,)), ((), ())), preferred_element_type=F32
    )


def norm_stats(rows):
    centre = jnp.mean(rows, axis=-1, keepdims=True)
    centred = rows - centre
    spread = jnp.mean(centred * centred, axis=-1, keepdims=True)
    scale = lax.rsqrt(spread + norm_eps)
    return centred * scale, scale


def norm_back(d_normed, gain_row, hat, scale):
    d_hat = d_normed * gain_row
    mean_d = jnp.mean(d_hat, axis=-1, keepdims=True)
    mean_dh = jnp.mean(d_hat * hat, axis=-1, keepdims=True)
    return scale * (d_hat - mean_d - hat * mean_dh)


class Sizes:
    def __init__(self, n_f, rows, width, ff, group, buckets, heads):
        self.n_f = n_f
        self.half = n_f // 2
        self.rows = rows
        self.width = width
        self.ff = ff
        self.group = group
        self.buckets = buckets
        self.heads = heads
        self.head = width // heads
        self.w_rows = width // n_f
        self.d_rows = ff // n_f
        self.own_ff = ff // CTX
        self.part = self.d_rows // CTX
        self.owned = n_f // CTX
        self.blocks = CTX * (CTX + 1) // 2


class Links:
    def __init__(self, send_sems, recv_sems):
        self.send_sems = send_sems
        self.recv_sems = recv_sems
        self.used = 0
        self.pending = []

    def copy(self, src, dst, index, arrival, device):
        return pltpu.make_async_remote_copy(
            src_ref=src,
            dst_ref=dst,
            send_sem=self.send_sems.at[index],
            recv_sem=self.recv_sems.at[arrival],
            device_id=device,
            device_id_type=MESH,
        )

    def send(self, src, dst, arrival, device):
        self.copy(src, dst, self.used, arrival, device).start()
        self.pending.append((src, self.used, device))
        self.used += 1

    def send_all(self, pairs, arrival, devices, size):
        for (src, dst), device in zip(pairs, devices):
            self.copy(src, dst, self.used, arrival, device).start()
        self.pending.append((size, self.used, devices[0]))
        self.used += 1

    def wait(self, dst, arrival, device):
        self.copy(dst, dst, 0, arrival, device).wait_recv()

    def drain(self):
        for src, index, device in self.pending:
            self.copy(src, src, index, 0, device).wait_send()
        self.pending = []


SENDS = 128


def layer_kernel(
    sizes,
    tok_in,
    seg_in,
    table_in,
    wqkv_in,
    wout_in,
    win_in,
    wdown_in,
    vec_in0,
    vec_in1,
    vec_in2,
    vec_in3,
    vec_in4,
    bias_in_in,
    rel_in,
    dy_in,
    out_ref,
    dx_ref,
    gqk_ref,
    gv_ref,
    gout_ref,
    gin_ref,
    gdown_ref,
    small_ref,
    *scratch_refs,
):
    s, sem = name_scratch(scratch_spec(sizes), scratch_refs[:-3])
    send_sems, recv_sems, own_sems = scratch_refs[-3:]
    n_f, half, rows = sizes.n_f, sizes.half, sizes.rows
    width, w_rows, d_rows, own_ff = sizes.width, sizes.w_rows, sizes.d_rows, sizes.own_ff
    part, out_part = sizes.part, sizes.w_rows // CTX
    head = sizes.head

    c = lax.axis_index("ctx")
    f = lax.axis_index("fsdp")
    side = c // 2
    core = c % 2
    place = f // 2
    par = f % 2
    sib = side * 2 + 1 - core
    opp = (1 - side) * 2 + core
    diag = (1 - side) * 2 + 1 - core

    def ctx_dev(index):
        return {"ctx": index, "fsdp": f}

    def f_dev(index):
        return {"ctx": c, "fsdp": index}

    partner = 2 * place + 1 - par

    def other_place(step):
        return lax.rem(place + step, half)

    links = Links(send_sems, recv_sems)

    barrier = pltpu.get_barrier_semaphore()
    for step in range(1, CTX):
        pl.semaphore_signal(
            barrier, inc=1, device_id=ctx_dev(lax.rem(c + step, CTX)), device_id_type=MESH
        )
    for step in range(1, n_f):
        pl.semaphore_signal(
            barrier, inc=1, device_id=f_dev(lax.rem(f + step, n_f)), device_id_type=MESH
        )

    own_copies, leaving = [], []

    def fetch(src, dst):
        made = pltpu.make_async_copy(src, dst, own_sems.at[len(own_copies)])
        own_copies.append(made)
        made.start()
        return made

    def keep(src, dst):
        made = pltpu.make_async_copy(src, dst, own_sems.at[len(own_copies)])
        own_copies.append(made)
        made.start()
        leaving.append(made)

    first_fetches = []
    for third in range(3):
        cols = pl.ds(pl.multiple_of(third * width + c * LANES, LANES), LANES)
        first_fetches.append(
            fetch(wqkv_in.at[:, cols], s.wq.at[f, :, third * LANES : (third + 1) * LANES])
        )
    first_fetches.append(fetch(tok_in, s.tok.at[c]))
    own_block = pl.ds(pl.multiple_of(c * LANES, LANES), LANES)
    later_fetches = [
        fetch(wdown_in.at[pl.ds(pl.multiple_of(c * part, 8), part), :], s.wd.at[f]),
        fetch(wout_in.at[:, own_block], s.wo.at[c, f]),
        fetch(dy_in, s.dy.at[c]),
    ]
    small_in = (vec_in0, vec_in1, vec_in2, vec_in3, vec_in4)
    small_fetches = [fetch(ref, s.ones[at]) for at, ref in enumerate(small_in)]
    small_fetches.append(fetch(bias_in_in, s.bias))
    table_fetches = [fetch(seg_in, s.seg), fetch(table_in, s.table), fetch(rel_in, s.rel)]
    hidden_fetch = fetch(win_in, s.win)
    for made in small_fetches:
        made.wait()
    for at in range(len(small_in)):
        s.vec[f, at : at + 1, 0:w_rows] = s.ones[at][...].astype(F32)
    for at in range(s.bias.shape[0]):
        size = s.bias.shape[1]
        s.vec[f, 5:6, at * size : (at + 1) * size] = s.bias[at : at + 1, :].astype(F32)
    hidden_fetch.wait()
    for at in range(CTX):

        @pl.when(c == at)
        def pick_hidden(at=at):
            starts = [index * d_rows + at * part for index in range(n_f)]
            s.wi[f] = jnp.concatenate([s.win[:, low : low + part] for low in starts], axis=1)

    for made in first_fetches + table_fetches:
        made.wait()

    pl.semaphore_wait(barrier, CTX - 1 + n_f - 1)

    peers = [f_dev(lax.rem(f + step, n_f)) for step in range(1, n_f)]
    far = [2 * other_place(step) + par for step in range(1, half)]
    others = [ctx_dev(lax.rem(c + step, CTX)) for step in range(1, CTX)]

    def to_peers(buf, first):
        piece = buf.at[f]
        links.send_all([(piece, piece)] * (n_f - 1), first, peers, buf.at[0 : n_f - 1])

    def from_peers(buf, first):
        links.wait(buf.at[0 : n_f - 1], first, peers[0])

    def to_group(buf, first):
        piece = buf.at[c]
        links.send_all([(piece, piece)] * (CTX - 1), first, others, buf.at[0 : CTX - 1])

    def from_group(buf, first):
        links.wait(buf.at[0 : CTX - 1], first, others[0])

    def spread(buf, first):
        piece = buf.at[f]
        links.send_all(
            [(piece, piece)] * (half - 1),
            first[0] + place,
            [f_dev(to) for to in far],
            buf.at[0 : half - 1],
        )
        links.send(piece, piece, first[1], f_dev(partner))

    def pass_on(buf, first):
        pairs = []
        for step in range(1, half):
            src = far[step - 1]
            links.wait(buf.at[src], first[0] + src // 2, f_dev(src))
            links.send(buf.at[src], buf.at[src], first[1], f_dev(partner))

    def settle(buf, first):
        links.wait(buf.at[0:half], first[1], f_dev(partner))

    for to in (sib, opp):
        links.send(s.tok.at[c], s.tok.at[c], sem.tok + c, ctx_dev(to))
    to_peers(s.vec, sem.vec)
    spread(s.wq, sem.wq)
    for made in later_fetches:
        made.wait()
    own_out = s.wo.at[c]

    ids = lax.broadcasted_iota(jnp.int32, (sizes.buckets, sizes.group), 0)
    onehot = (ids == s.table[...]).astype(BF16)
    s.hot[...] = onehot.astype(F32)
    s.bvec[...] = mm(s.rel[...], onehot)
    for h in range(2):
        row = s.bvec[pl.ds(2 * c + h, 1), :]
        for delta in range(CTX):
            now = row[:, delta * rows : (delta + 1) * rows]
            before = row[:, (delta - 1) * rows : delta * rows] if delta else now
            wide = jnp.broadcast_to(jnp.concatenate([now, before], axis=1), (rows, 2 * rows))
            turned = pltpu.roll(wide, 0, 1, stride=1, stride_axis=0)
            s.tile[h, delta] = turned[:, :rows]
    seg_f = s.seg[...].astype(F32)
    for at in range(CTX):
        piece = jnp.broadcast_to(seg_f[:, at * rows : (at + 1) * rows], (rows, rows))
        s.segk[at] = jnp.transpose(piece)
    key_pos = lax.broadcasted_iota(jnp.int32, (rows, rows), 0)
    query_pos = lax.broadcasted_iota(jnp.int32, (rows, rows), 1)
    for q_at in range(CTX):
        seg_q = jnp.broadcast_to(seg_f[:, q_at * rows : (q_at + 1) * rows], (rows, rows))
        for k_at in range(q_at + 1):
            seg_k = s.segk[k_at]
            allowed = (seg_k == 0.0) | (seg_k == seg_q)
            if q_at == k_at:
                allowed = allowed & (key_pos <= query_pos)
            for h in range(2):
                block = q_at * (q_at + 1) // 2 + k_at
                s.bm[h, block] = jnp.where(allowed, s.tile[h, q_at - k_at], masked_low)

    from_peers(s.vec, sem.vec)

    def joined(pieces, count, size):
        total = count * size
        spot = lax.broadcasted_iota(jnp.int32, (size, total), 1) % size
        which = lax.broadcasted_iota(jnp.int32, (size, total), 0)
        spreader = (spot == which).astype(BF16)
        flat = mm(pieces.astype(BF16), spreader)
        owner = lax.broadcasted_iota(jnp.int32, (count, total), 1) // size
        mine = owner == lax.broadcasted_iota(jnp.int32, (count, total), 0)
        return jnp.sum(jnp.where(mine, flat, 0.0), axis=0, keepdims=True)

    for at in range(5):
        s.vrow[at : at + 1, :] = joined(s.vec[:, at, 0:w_rows], n_f, w_rows)
    for at in range(CTX):

        @pl.when(c == at)
        def pick_bias(at=at):
            s.vrow[5:6, :] = joined(s.vec[:, 5, at * part : (at + 1) * part], n_f, part)

    gain_one, shift_one = s.vrow[0:1, :], s.vrow[1:2, :]
    gain_two, shift_two = s.vrow[2:3, :], s.vrow[3:4, :]
    bias_down_row, bias_in_row = s.vrow[4:5, :], s.vrow[5:6, :]

    step_rows = 64

    def row_loop(body, count=rows):
        def run(at, carried):
            body(pl.ds(pl.multiple_of(at * step_rows, step_rows), step_rows))
            return carried

        lax.fori_loop(0, count // step_rows, run, 0)

    def first_norm(chunk):
        def body(part):
            hat, scale = norm_stats(s.tok[chunk, part, :].astype(F32))
            s.fn[chunk, part, :] = (hat * gain_one + shift_one).astype(BF16)

        row_loop(body)

    def whole(buf, count, size, kept):
        if size % 16 == 0:
            return buf[...].reshape(count * size, buf.shape[2])
        for at in range(count):
            kept[at * size : (at + 1) * size, :] = buf[at]
        return kept[...]

    head_rows = lax.broadcasted_iota(jnp.int32, (LANES, rows), 0) // head

    def project(chunk):
        weights = whole(s.wq, n_f, w_rows, s.flat_wq)
        made = mm(s.fn[chunk], weights)
        queries = made[:, 0:LANES].astype(BF16).astype(F32) * (head ** -0.5)
        keys = made[:, LANES : 2 * LANES]
        values = made[:, 2 * LANES : 3 * LANES]
        s.k[chunk] = keys.astype(BF16)
        s.v[chunk] = values.astype(BF16)
        s.kt[chunk] = jnp.transpose(keys).astype(BF16)
        s.vt[chunk] = jnp.transpose(values).astype(BF16)
        turned = jnp.transpose(queries)
        for h in range(2):
            kept = jnp.where(head_rows == h, turned, 0.0)
            s.qt[h, chunk] = kept.astype(BF16)
            s.q[h, chunk] = jnp.transpose(kept).astype(BF16)

    first_norm(c)
    pass_on(s.wq, sem.wq)
    to_peers(own_out, sem.wo[0])
    spread(s.wi, sem.wi)
    spread(s.wd, sem.wd)
    links.wait(s.tok.at[sib], sem.tok + sib, ctx_dev(sib))
    first_norm(sib)
    links.wait(s.tok.at[opp], sem.tok + opp, ctx_dev(opp))
    links.send(s.tok.at[opp], s.tok.at[opp], sem.tok + opp, ctx_dev(sib))
    first_norm(opp)

    for to in (sib, opp):
        links.send(s.dy.at[c], s.dy.at[c], sem.dy + c, ctx_dev(to))

    def share_out(to, block):
        links.send(s.wo.at[block], s.wo.at[block], sem.wo[1] + block, ctx_dev(to))

    def wait_out(block, via):
        links.wait(s.wo.at[block], sem.wo[1] + block, ctx_dev(via))

    settle(s.wq, sem.wq)
    project(c)
    project(sib)
    project(opp)
    links.wait(s.tok.at[diag], sem.tok + diag, ctx_dev(sib))
    first_norm(diag)
    project(diag)
    from_peers(own_out, sem.wo[0])
    share_out(sib, c)
    share_out(opp, c)

    def attend_rows(chunk):
        first_block = chunk * (chunk + 1) // 2
        for h in range(2):
            top = jnp.full((1, rows), masked_low, F32)
            for k_at in range(chunk + 1):
                scores = mm(s.k[k_at], s.qt[h, chunk]) + s.bm[h, first_block + k_at]
                s.sc[h, k_at] = scores
                top = jnp.maximum(top, jnp.max(scores, axis=0, keepdims=True))
            lanes = slice(h * head, (h + 1) * head)
            total = jnp.zeros((1, rows), F32)
            mixed = jnp.zeros((head, rows), F32)
            for k_at in range(chunk + 1):
                weights = jnp.exp(s.sc[h, k_at] - top)
                total = total + jnp.sum(weights, axis=0, keepdims=True)
                rounded = weights.astype(BF16)
                s.e[h, first_block + k_at] = rounded
                mixed = mixed + mm(s.vt[k_at, lanes, :], rounded)
            inverse = 1.0 / total
            s.linv[chunk, h : h + 1, :] = inverse
            s.att_t[chunk, lanes, :] = mixed * inverse
        s.att[c, chunk] = jnp.transpose(s.att_t[chunk]).astype(BF16)

    def attend(turn):
        for which in range(2):
            pl.when(side == which)(functools.partial(attend_rows, (2 * which + turn) % CTX))

    def att_slot(owner, chunk):
        return owner * CTX + chunk

    def send_att(chunk):
        piece = s.att.at[c, chunk]
        for to in (sib, opp):
            links.send(piece, piece, sem.att + att_slot(c, chunk), ctx_dev(to))

    def wait_att(owner, chunk, via):
        links.wait(s.att.at[owner, chunk], sem.att + att_slot(owner, chunk), ctx_dev(via))

    def pass_att(chunk):
        wait_att(opp, chunk, opp)
        piece = s.att.at[opp, chunk]
        links.send(piece, piece, sem.att + att_slot(opp, chunk), ctx_dev(sib))

    mine = [lax.rem(2 * side + step, CTX) for step in range(CTX)]
    theirs = [lax.rem(2 * (1 - side) + step, CTX) for step in range(CTX)]
    attend(0)
    send_att(mine[0])
    attend(1)
    send_att(mine[1])
    pass_on(s.wi, sem.wi)
    pass_att(theirs[0])
    wait_out(opp, opp)
    share_out(sib, opp)
    attend(2)
    send_att(mine[2])
    pass_on(s.wd, sem.wd)
    pass_att(theirs[1])
    links.wait(s.dy.at[opp], sem.dy + opp, ctx_dev(opp))
    links.send(s.dy.at[opp], s.dy.at[opp], sem.dy + opp, ctx_dev(sib))
    attend(3)
    send_att(mine[3])

    wait_out(sib, sib)
    wait_out(diag, sib)
    for block in range(CTX):
        cols = slice(block * LANES, (block + 1) * LANES)
        if w_rows % 16 == 0:
            s.wo_flat[:, cols] = s.wo[block].reshape(width, LANES)
        else:
            for at in range(n_f):
                s.wo_flat[at * w_rows : (at + 1) * w_rows, cols] = s.wo[block, at]

    def gather_att(chunk):
        wait_att(sib, chunk, sib)
        wait_att(diag, chunk, sib)

    def feed(chunk):
        gather_att(chunk)
        mixed = jnp.zeros((rows, width), F32)
        for owner in range(CTX):
            mixed += mm(
                s.att[owner, chunk], s.wo_flat[owner * LANES : (owner + 1) * LANES, :]
            )
        s.mid[...] = mixed + s.tok[chunk].astype(F32)

        def normed(rng):
            hat, scale = norm_stats(s.mid[rng, :])
            s.sn[chunk, rng, :] = (hat * gain_two + shift_two).astype(BF16)

        row_loop(normed)
        s.inner[chunk] = mm(s.sn[chunk], whole(s.wi, n_f, w_rows, s.flat_wi))

    def feed_back(chunk):
        w_down = whole(s.wd, n_f, part, s.flat_wd)
        s.dact[...] = mm(s.dy[chunk], w_down, 1, 1)

        def gelu(rng):
            inner = s.inner[chunk, rng, :] + bias_in_row
            phi = 0.5 + 0.5 * lax.erf(inner * (2.0 ** -0.5))
            slope = phi + inner * (jnp.exp(-0.5 * inner * inner) * (1.0 / math.sqrt(2.0 * math.pi)))
            s.actv[chunk, rng, :] = (inner * phi).astype(BF16)
            s.din[chunk, rng, :] = (s.dact[rng, :] * slope).astype(BF16)

        row_loop(gelu)
        return mm(s.din[chunk], whole(s.wi, n_f, w_rows, s.flat_wi), 1, 1)

    def scatter_first(group, first, part):
        group[0][...] = part.astype(BF16)
        links.send(group[0], group[1], first[0], ctx_dev(sib))

    def scatter_second(group, first, part):
        links.wait(group[1], first[0], ctx_dev(sib))
        group[2][...] = (part + group[1][...].astype(F32)).astype(BF16)
        links.send(group[2], group[3], first[1], ctx_dev(opp))

    def scatter_third(group, first, part):
        group[4][...] = part.astype(BF16)
        links.send(group[4], group[5], first[2], ctx_dev(sib))

    def scatter_wait(group, first):
        links.wait(group[5], first[2], ctx_dev(sib))
        links.wait(group[3], first[1], ctx_dev(opp))

    def scatter_sum(group, part):
        return group[3][part, :].astype(F32) + group[5][part, :].astype(F32)

    settle(s.wi, sem.wi)
    feed(diag)
    pass_att(theirs[2])
    feed(opp)
    pass_att(theirs[3])
    feed(sib)
    feed(c)
    settle(s.wd, sem.wd)
    links.wait(s.dy.at[diag], sem.dy + diag, ctx_dev(sib))
    scatter_first(s.rs_s, sem.rs_s, feed_back(diag))
    scatter_second(s.rs_s, sem.rs_s, feed_back(opp))
    links.wait(s.dy.at[sib], sem.dy + sib, ctx_dev(sib))
    scatter_third(s.rs_s, sem.rs_s, feed_back(sib))
    s.dsec[...] = feed_back(c)

    def even_pieces(group, left, right, cols, size):
        for at in range(left.shape[2] // LANES):
            lhs = left[:, :, at * LANES : (at + 1) * LANES].reshape(CTX * rows, LANES)
            made = mm(lhs, right[...].reshape(CTX * rows, cols), 0, 0).astype(BF16)
            for piece in range(LANES // size):
                to = at * (LANES // size) + piece
                group[0][to % 2, to // 2] = made[piece * size : (piece + 1) * size, :]

    def grad_pair(group, first):
        for to in far:
            links.send(
                group[0].at[1 - par, to // 2], group[1].at[to // 2], first[0] + to // 2, f_dev(partner)
            )
        links.send(group[0].at[1 - par, place], group[1].at[place], first[0] + place, f_dev(partner))

    def grad_step(group, first, step):
        at = far[step] // 2 if step < half - 1 else place
        links.wait(group[1].at[at], first[0] + at, f_dev(partner))
        group[2][at] = (group[0][par, at].astype(F32) + group[1][at].astype(F32)).astype(BF16)
        if step < half - 1:
            links.send(group[2].at[at], group[3].at[place], first[1], f_dev(far[step]))

    def grad_steps(group, first, low=0, high=half):
        for step in range(low, high):
            grad_step(group, first, step)

    def grad_even_third(group, first):
        links.wait(group[3].at[0 : half - 1], first[1], f_dev(far[0]))
        total = group[2][place].astype(F32)
        for src in far:
            total += group[3][src // 2].astype(F32)
        group[4][c] = total.astype(BF16)
        to_group(group[4], first[2])

    def grad_direct(group, first):
        pairs = [
            (group[0].at[lax.rem(f + step, n_f)], group[1].at[f]) for step in range(1, n_f)
        ]
        links.send_all(pairs, first[0], peers, group[1].at[0 : n_f - 1])

    def grad_direct_sum(group, first):
        from_peers(group[1], first[0])
        total = group[0][f].astype(F32)
        for step in range(1, n_f):
            total += group[1][lax.rem(f + step, n_f)].astype(F32)
        group[2][c] = total.astype(BF16)
        to_group(group[2], first[1])

    even_pieces(s.gd, s.actv, s.dy, width, part)
    grad_pair(s.gd, sem.gd)
    even_pieces(s.gi, s.sn, s.din, own_ff, w_rows)
    grad_pair(s.gi, sem.gi)
    w_down = whole(s.wd, n_f, part, s.flat_wd)
    scatter_first(s.rs_o, sem.rs_o, mm(s.actv[diag], w_down))
    scatter_third(s.rs_o, sem.rs_o, mm(s.actv[sib], w_down))
    grad_steps(s.gd, sem.gd, 0, half // 2)

    scatter_wait(s.rs_s, sem.rs_s)
    s.vg[...] = jnp.zeros_like(s.vg)

    def second_back(rng):
        hat, scale = norm_stats(s.mid[rng, :])
        d_second = s.dsec[rng, :] + scatter_sum(s.rs_s, rng)
        d_result = s.dy[c, rng, :].astype(F32)
        d_middle = d_result + norm_back(d_second, gain_two, hat, scale)
        s.dmid[rng, :] = d_middle
        s.dmx[rng, :] = d_middle.astype(BF16)
        s.vg[2:3, :] += jnp.sum(d_second * hat, axis=0, keepdims=True)
        s.vg[3:4, :] += jnp.sum(d_second, axis=0, keepdims=True)
        s.vg[4:5, :] += jnp.sum(d_result, axis=0, keepdims=True)

    row_loop(second_back)
    d_att = mm(s.wo_flat[...], s.dmx[...], 1, 1)
    s.dat_out[...] = d_att.astype(BF16).reshape(CTX, LANES, rows)
    for to in (opp, diag, sib):
        links.send(s.dat_out.at[to], s.dat.at[c], sem.dat + c, ctx_dev(to))
    s.dat[c] = s.dat_out[c]
    for owner in range(CTX):
        made = mm(s.att[owner, c], s.dmx[...], 0, 0).astype(BF16)
        for piece in range(LANES // w_rows):
            at = owner * (LANES // w_rows) + piece
            for part_at in range(CTX):
                low = piece * w_rows + part_at * out_part
                s.go_own[part_at % 2, part_at // 2, at] = made[low : low + out_part, :]
    links.send(s.go_own.at[1 - core], s.go_core, sem.go_core, ctx_dev(sib))
    grad_steps(s.gd, sem.gd, half // 2, half)
    links.wait(s.go_core, sem.go_core, ctx_dev(sib))
    s.go_two[...] = (
        s.go_own[core].astype(F32) + s.go_core[...].astype(F32)
    ).astype(BF16)
    links.send(s.go_two.at[1 - side], s.go_side, sem.go_side, ctx_dev(opp))
    scatter_second(s.rs_o, sem.rs_o, mm(s.actv[opp], w_down))
    s.outp[...] = s.mid[...] + mm(s.actv[c], w_down) + bias_down_row
    for at in range(CTX):

        def bias_rows(rng, at=at):
            s.vg[5:6, :] += jnp.sum(s.din[at, rng, :].astype(F32), axis=0, keepdims=True)

        row_loop(bias_rows)
    grad_steps(s.gi, sem.gi, 0, half // 2)

    for src in (sib, opp, diag):
        links.wait(s.dat.at[src], sem.dat + src, ctx_dev(src))
    for at in range(CTX):
        got = s.dat[at].astype(F32)
        for h in range(2):
            part = slice(h * head, (h + 1) * head)
            scaled = (got * s.linv[at, h : h + 1, :]).astype(BF16)
            kept = jnp.where(head_rows == h, scaled.astype(F32), 0.0)
            s.dat_t[h, at] = kept.astype(BF16)
            s.dat_n[h, at] = jnp.transpose(kept).astype(BF16)
            s.delta[at, h : h + 1, :] = jnp.sum(
                kept[part, :] * s.att_t[at, part, :], axis=0, keepdims=True
            )
        s.dqt[at] = jnp.zeros((LANES, rows), F32)
        s.dk[at] = jnp.zeros((rows, LANES), F32)
    s.dbm[...] = jnp.zeros_like(s.dbm)

    def block_pair(q_at, k_at):
        block = q_at * (q_at + 1) // 2 + k_at
        values = s.v[k_at]
        for h in range(2):
            lanes = slice(h * head, (h + 1) * head)
            d_probs = mm(values, s.dat_t[h, q_at])
            rounded = s.e[h, block]
            d_scores = rounded.astype(F32) * (d_probs - s.delta[q_at, h : h + 1, :])
            s.dbm[h, q_at - k_at] += d_scores
            low = d_scores.astype(BF16)
            s.dk[k_at] += mm(low, s.q[h, q_at])
            s.dqt[q_at, lanes, :] += mm(s.kt[k_at, lanes, :], low)

    def query_row(upper):
        def run(lower, carried):
            shift = side * (CTX - 1 - upper - lower)
            block_pair(upper + shift, lower + shift)
            return carried

        lax.fori_loop(0, upper + 1, run, 0)

    def pack(chunk):
        s.dp[chunk, :, 0:LANES] = (jnp.transpose(s.dqt[chunk]) * (head ** -0.5)).astype(BF16)
        s.dp[chunk, :, LANES : 2 * LANES] = s.dk[chunk].astype(BF16)

    w_qkv = whole(s.wq, n_f, w_rows, s.flat_wq)

    def back_first(chunk):
        s.dsec[...] = mm(s.dp[chunk], w_qkv, 1, 1)

        def add_rows(rng):
            part_rows = s.dsec[rng, :]
            s.vg[0:1, :] += jnp.sum(s.fn[chunk, rng, :].astype(F32) * part_rows, axis=0, keepdims=True)
            s.vg[1:2, :] += jnp.sum(part_rows, axis=0, keepdims=True)

        return add_rows

    def value_grads(k_at):
        made = jnp.zeros((rows, LANES), F32)
        for q_at in range(k_at, CTX):
            block = q_at * (q_at + 1) // 2 + k_at
            for h in range(2):
                made += mm(s.e[h, block], s.dat_n[h, q_at])
        s.dp[k_at, :, 2 * LANES : 3 * LANES] = made.astype(BF16)

    def qkv_pieces(group, cols):
        for at in range(width // LANES):
            lhs = s.fn[:, :, at * LANES : (at + 1) * LANES].reshape(CTX * rows, LANES)
            rhs = s.dp[:, :, cols].reshape(CTX * rows, cols.stop - cols.start)
            made = mm(lhs, rhs, 0, 0).astype(BF16)
            for piece in range(LANES // w_rows):
                to = at * (LANES // w_rows) + piece
                got = made[piece * w_rows : (piece + 1) * w_rows, :]
                if len(group) == 5:
                    group[0][to % 2, to // 2] = got
                else:
                    group[0][to] = got

    for at in range(CTX):
        value_grads(at)
    qkv_pieces(s.gv, slice(2 * LANES, 3 * LANES))
    grad_pair(s.gv, sem.gv)
    query_row(3)
    grad_steps(s.gi, sem.gi, half // 2, half)
    links.wait(s.go_side, sem.go_side, ctx_dev(opp))
    for at in range(n_f):
        s.go[0][at % 2, at // 2] = (
            s.go_two[side, at].astype(F32) + s.go_side[at].astype(F32)
        ).astype(BF16)
    grad_pair(s.go, sem.go)
    query_row(2)
    pack(diag)
    pack(opp)
    sums = back_first(diag)
    scatter_first(s.rs_f, sem.rs_f, s.dsec[...])
    row_loop(sums)
    sums = back_first(opp)
    scatter_second(s.rs_f, sem.rs_f, s.dsec[...])
    row_loop(sums)
    grad_steps(s.gv, sem.gv)
    query_row(1)
    grad_steps(s.go, sem.go)
    query_row(0)
    pack(sib)
    pack(c)
    qkv_pieces(s.gq, slice(0, 2 * LANES))
    grad_direct(s.gq, sem.gq)
    grad_even_third(s.gv, sem.gv)
    sums = back_first(sib)
    scatter_third(s.rs_f, sem.rs_f, s.dsec[...])
    row_loop(sums)
    sums = back_first(c)
    row_loop(sums)

    for h in range(2):
        pieces = []
        for delta in range(CTX):
            block = s.dbm[h, delta]
            wide = jnp.concatenate([block, jnp.zeros((rows, rows), F32)], axis=1)
            count = rows
            while count > 1:
                count //= 2
                turned = pltpu.roll(wide[count : 2 * count, :], 2 * rows - count, 1)
                wide = wide[0:count, :] + turned
            pieces.append(wide)
        total = []
        for delta in range(CTX):
            here = pieces[delta][:, 0:rows]
            if delta + 1 < CTX:
                here = here + pieces[delta + 1][:, rows : 2 * rows]
            total.append(here)
        dist = jnp.concatenate(total, axis=1)
        bucket_sums = lax.dot_general(
            jnp.broadcast_to(dist, (8, sizes.group)),
            s.hot[...],
            (((1,), (1,)), ((), ())),
            preferred_element_type=F32,
            precision=lax.Precision.HIGHEST,
        )
        s.vg[6 + h : 7 + h, 0 : sizes.buckets] = bucket_sums[0:1, :]

    s.vg[0:1, :] = (s.vg[0:1, :] - shift_one * s.vg[1:2, :]) / gain_one
    for to in range(n_f):
        s.vgp[to, :, 0:w_rows] = s.vg[:, to * w_rows : (to + 1) * w_rows]
        s.vgp[to, 6:8, 0 : sizes.buckets] = s.vg[6:8, 0 : sizes.buckets]
    pairs = [(s.vgp.at[lax.rem(f + step, n_f)], s.vgf.at[f]) for step in range(1, n_f)]
    links.send_all(pairs, sem.vgf, peers, s.vgf.at[0 : n_f - 1])

    grad_even_third(s.gd, sem.gd)
    scatter_wait(s.rs_f, sem.rs_f)

    def first_back(rng):
        hat, scale = norm_stats(s.tok[c, rng, :].astype(F32))
        d_first = s.dsec[rng, :] + scatter_sum(s.rs_f, rng)
        d_x = s.dmid[rng, :] + norm_back(d_first, gain_one, hat, scale)
        s.dx[rng, :] = d_x.astype(BF16)

    row_loop(first_back)
    keep(s.dx, dx_ref)
    grad_direct_sum(s.gq, sem.gq)
    from_peers(s.vgf, sem.vgf)
    total = s.vgp[f]
    for step in range(1, n_f):
        total += s.vgf[lax.rem(f + step, n_f)]
    s.vgc[c] = total
    to_group(s.vgc, sem.vgc)
    grad_even_third(s.go, sem.go)
    grad_even_third(s.gi, sem.gi)

    scatter_wait(s.rs_o, sem.rs_o)
    s.out[...] = (
        s.outp[...] + s.rs_o[3][...].astype(F32) + s.rs_o[5][...].astype(F32)
    ).astype(BF16)
    keep(s.out, out_ref)
    from_group(s.gd[4], sem.gd[2])
    keep(s.gd[4], gdown_ref)
    from_group(s.gv[4], sem.gv[2])
    keep(s.gv[4], gv_ref)
    from_group(s.gq[2], sem.gq[1])
    keep(s.gq[2], gqk_ref)
    from_group(s.vgc, sem.vgc)
    keep(s.vgc, small_ref)
    from_group(s.go[4], sem.go[2])
    keep(s.go[4], gout_ref)
    from_group(s.gi[4], sem.gi[2])
    keep(s.gi[4], gin_ref)
    links.drain()
    for made in leaving:
        made.wait()


def finish_kernel(
    sizes,
    out_in,
    dx_in,
    gqk_in,
    gv_in,
    gout_in,
    gin_in,
    gdown_in,
    small_in,
    out_ref,
    dx_ref,
    gqkv_ref,
    gout_ref,
    gin_ref,
    gdown_ref,
    gg1_ref,
    gs1_ref,
    gg2_ref,
    gs2_ref,
    gbi_ref,
    gbd_ref,
    grel_ref,
    gqkv,
    gout,
    gin,
    gdown,
    gqk_low,
    gv_low,
    gout_low,
    gin_low,
    gdown_low,
    out_low,
    dx_low,
    sems,
):
    made = []

    def start(src, dst):
        copy = pltpu.make_async_copy(src, dst, sems.at[len(made)])
        copy.start()
        made.append(copy)
        return copy

    loads = [
        start(gdown_in, gdown_low),
        start(gin_in, gin_low),
        start(gqk_in, gqk_low),
        start(gout_in, gout_low),
    ]
    loads += [start(out_in, out_low), start(dx_in, dx_low), start(gv_in, gv_low)]
    width, own_ff = sizes.width, sizes.own_ff
    loads[0].wait()
    for at in range(CTX):
        gdown[at * sizes.part : (at + 1) * sizes.part, :] = gdown_low[at].astype(F32)
    stores = [start(gdown, gdown_ref)]
    loads[1].wait()
    part = sizes.part
    for index in range(sizes.n_f):
        lanes = slice(index * part, (index + 1) * part)
        joined = jnp.concatenate([gin_low[at, :, lanes].astype(F32) for at in range(CTX)], axis=1)
        gin[:, index * CTX * part : (index + 1) * CTX * part] = joined
    stores.append(start(gin, gin_ref))
    loads[2].wait()
    loads[6].wait()
    for at in range(CTX):
        for third in range(3):
            low = third * width + at * LANES
            if third == 2:
                got = gv_low[at]
            else:
                got = gqk_low[at, :, third * LANES : (third + 1) * LANES]
            gqkv[:, low : low + LANES] = got.astype(F32)
    stores.append(start(gqkv, gqkv_ref))
    loads[3].wait()
    out_part = sizes.w_rows // CTX
    for at in range(CTX):
        gout[at * out_part : (at + 1) * out_part, :] = gout_low[at].astype(F32)
    stores.append(start(gout, gout_ref))
    loads[4].wait()
    stores.append(start(out_low, out_ref))
    loads[5].wait()
    stores.append(start(dx_low, dx_ref))
    total = jnp.sum(small_in[...], axis=0)
    for at, ref in enumerate((gg1_ref, gs1_ref, gg2_ref, gs2_ref, gbd_ref)):
        ref[...] = total[at : at + 1, 0 : sizes.w_rows]
    size = gbi_ref.shape[1]
    hidden = jnp.concatenate([small_in[at, 5:6, 0 : sizes.part] for at in range(CTX)], axis=1)
    for at in range(gbi_ref.shape[0]):
        gbi_ref[at : at + 1, :] = hidden[:, at * size : (at + 1) * size]
    for at in range(CTX):
        grel_ref[2 * at : 2 * at + 2, :] = small_in[at, 6:8, 0 : sizes.buckets]
    for copy in stores:
        copy.wait()


def scratch_spec(z):
    rows, width, group = z.rows, z.width, z.group
    blocks = CTX * (CTX + 1) // 2
    act = (CTX, rows, width)
    hidden = (CTX, rows, z.own_ff)
    tall = (CTX, rows, LANES)
    wide = (CTX, LANES, rows)
    squares = (2, CTX, rows, rows)

    def scatter():
        flat = ((rows, width), BF16)
        landing = ((rows, width), BF16, 1)
        return [flat, landing, flat, landing, flat, landing]

    def even(size, cols):
        part = (z.half, size, cols)
        return [
            ((2,) + part, BF16),
            (part, BF16, z.half),
            (part, BF16),
            (part, BF16, 1),
            ((CTX, size, cols), BF16, 1),
        ]

    def direct(size, cols):
        whole = (z.n_f, size, cols)
        return [(whole, BF16), (whole, BF16, 1), ((CTX, size, cols), BF16, 1)]

    out_part = z.w_rows // CTX
    out_rows = (z.n_f, out_part, width)
    spec = dict(
        tok=(act, BF16, CTX),
        dy=(act, BF16, CTX),
        fn=(act, BF16),
        wq=((z.n_f, z.w_rows, 3 * LANES), BF16, z.half, 1),
        wo=((CTX, z.n_f, z.w_rows, LANES), BF16, 1, CTX),
        wo_flat=((width, width), BF16),
        wi=((z.n_f, z.w_rows, z.own_ff), BF16, z.half, 1),
        wd=((z.n_f, z.part, width), BF16, z.half, 1),
        vec=((z.n_f, 8, max(z.d_rows, LANES)), F32, 1),
        ones=[((1, z.w_rows), BF16)] * 5,
        bias=((max(1, z.d_rows // LANES), min(LANES, z.d_rows)), BF16),
        seg=((1, group), jnp.int32),
        table=((1, group), jnp.int32),
        rel=((z.heads, z.buckets), BF16),
        win=((z.w_rows, z.ff), BF16),
        out=((rows, width), BF16),
        dx=((rows, width), BF16),
        vrow=((8, width), F32),
        hot=((z.buckets, group), F32),
        bvec=((8, group), F32),
        tile=(squares, F32),
        segk=((CTX, rows, rows), F32),
        bm=((2, blocks, rows, rows), F32),
        k=(tall, BF16),
        v=(tall, BF16),
        kt=(wide, BF16),
        vt=(wide, BF16),
        qt=((2,) + wide, BF16),
        q=((2,) + tall, BF16),
        sc=(squares, F32),
        e=((2, blocks, rows, rows), BF16),
        acc=((LANES, rows), F32),
        linv=((CTX, 8, rows), F32),
        att_t=(wide, F32),
        att=((CTX,) + tall, BF16, CTX * CTX),
        mid=((rows, width), F32),
        sn=(act, BF16),
        inner=((CTX, rows, z.own_ff), F32),
        dact=((rows, z.own_ff), F32),
        actv=(hidden, BF16),
        din=(hidden, BF16),
        dsec=((rows, width), F32),
        outp=((rows, width), F32),
        dmid=((rows, width), F32),
        dmx=((rows, width), BF16),
        dat_out=(wide, BF16),
        dat=(wide, BF16, CTX),
        dat_t=((2,) + wide, BF16),
        dat_n=((2,) + tall, BF16),
        delta=((CTX, 8, rows), F32),
        dqt=(wide, F32),
        dbm=(squares, F32),
        dk=(tall, F32),
        dp=((CTX, rows, 3 * LANES), BF16),
        vg=((8, width), F32),
        vgp=((z.n_f, 8, LANES), F32),
        vgf=((z.n_f, 8, LANES), F32, 1),
        vgc=((CTX, 8, LANES), F32, 1),
        rs_s=scatter(),
        rs_o=scatter(),
        rs_f=scatter(),
        gq=direct(z.w_rows, 2 * LANES),
        gv=even(z.w_rows, LANES),
        gi=even(z.w_rows, z.own_ff),
        gd=even(z.part, width),
        go=even(out_part, width),
        go_own=((2, 2) + out_rows, BF16),
        go_core=((2,) + out_rows, BF16, 1),
        go_two=((2,) + out_rows, BF16),
        go_side=(out_rows, BF16, 1),
    )
    if z.w_rows % 16:
        spec.update(
            flat_wq=((width, 3 * LANES), BF16),
            flat_wi=((width, z.own_ff), BF16),
        )
    else:
        spec.update(flat_wq=((8, LANES), BF16), flat_wi=((8, LANES), BF16))
    flat_shape = (z.own_ff, width) if z.part % 16 else (8, LANES)
    spec.update(flat_wd=(flat_shape, BF16))
    return spec


def scratch_items(spec):
    for item in spec.values():
        if isinstance(item, list):
            yield from item
        else:
            yield item


def name_scratch(spec, refs):
    refs = iter(refs)
    by_name, first, used = {}, {}, 0
    for name, item in spec.items():
        entries = item if isinstance(item, list) else [item]
        held, starts = [], []
        for entry in entries:
            held.append(next(refs))
            for count in entry[2:]:
                starts.append(used)
                used += count
        by_name[name] = held if isinstance(item, list) else held[0]
        if starts:
            first[name] = starts if isinstance(item, list) or len(starts) > 1 else starts[0]
    return SimpleNamespace(**by_name), SimpleNamespace(**first)


def per_device(
    n_f,
    tokens,
    segment_ids,
    bucket_table,
    w_qkv,
    w_out,
    w_in,
    w_down,
    gain_one,
    shift_one,
    gain_two,
    shift_two,
    bias_in,
    bias_down,
    rel_bias,
    cotangent,
):
    sizes = Sizes(
        n_f,
        tokens.shape[1],
        tokens.shape[2],
        w_in.shape[1],
        segment_ids.shape[1],
        rel_bias.shape[0],
        rel_bias.shape[1],
    )
    rows, width, w_rows, d_rows = sizes.rows, sizes.width, sizes.w_rows, sizes.d_rows
    vmem = pl.BlockSpec(memory_space=pltpu.VMEM)
    far = pl.BlockSpec(memory_space=pltpu.HBM)
    spec = scratch_spec(sizes)
    n_recv = sum(sum(item[2:]) for item in scratch_items(spec))
    bias_shape = (max(1, d_rows // LANES), min(LANES, d_rows))
    shaped = jax.ShapeDtypeStruct
    made = pl.pallas_call(
        functools.partial(layer_kernel, sizes),
        out_shape=[
            shaped((rows, width), BF16),
            shaped((rows, width), BF16),
            shaped((CTX, w_rows, 2 * LANES), BF16),
            shaped((CTX, w_rows, LANES), BF16),
            shaped((CTX, w_rows // CTX, width), BF16),
            shaped((CTX, w_rows, sizes.own_ff), BF16),
            shaped((CTX, sizes.part, width), BF16),
            shaped((CTX, 8, LANES), F32),
        ],
        in_specs=[far] * 15,
        out_specs=[far] * 8,
        scratch_shapes=[pltpu.VMEM(item[0], item[1]) for item in scratch_items(spec)]
        + [
            pltpu.SemaphoreType.DMA((SENDS if n_f == 8 else 8 * n_f,)),
            pltpu.SemaphoreType.DMA((n_recv,)),
            pltpu.SemaphoreType.DMA((26,)),
        ],
        compiler_params=pltpu.CompilerParams(
            collective_id=0, has_side_effects=True, vmem_limit_bytes=60 * 1024 * 1024
        ),
        name="layer",
    )(
        tokens[0],
        segment_ids,
        bucket_table[None],
        w_qkv,
        w_out,
        w_in,
        w_down,
        gain_one[None],
        shift_one[None],
        gain_two[None],
        shift_two[None],
        bias_down[None],
        bias_in.reshape(bias_shape),
        jnp.transpose(rel_bias),
        cotangent[0],
    )
    outs = [
        ((rows, width), BF16),
        ((rows, width), BF16),
        ((w_rows, 3 * width), F32),
        ((w_rows, width), F32),
        ((w_rows, sizes.ff), F32),
        ((d_rows, width), F32),
        ((1, w_rows), F32),
        ((1, w_rows), F32),
        ((1, w_rows), F32),
        ((1, w_rows), F32),
        (bias_shape, F32),
        ((1, w_rows), F32),
        ((sizes.heads, sizes.buckets), F32),
    ]
    done = pl.pallas_call(
        functools.partial(finish_kernel, sizes),
        out_shape=[shaped(shape, kind) for shape, kind in outs],
        in_specs=[far] * 7 + [vmem],
        out_specs=[far] * 6 + [vmem] * 7,
        scratch_shapes=[pltpu.VMEM(shape, kind) for shape, kind in outs[2:6]]
        + [pltpu.VMEM(item.shape, item.dtype) for item in made[2:7] + made[0:2]]
        + [pltpu.SemaphoreType.DMA((14,))],
        compiler_params=pltpu.CompilerParams(vmem_limit_bytes=60 * 1024 * 1024),
        name="finish",
    )(*made)
    return (
        done[0][None],
        done[1][None],
        done[2],
        done[3],
        done[4],
        done[5],
        done[6][0],
        done[7][0],
        done[8][0],
        done[9][0],
        done[10].reshape(-1),
        done[11][0],
        jnp.transpose(done[12]),
    )


def solution(mesh):
    by_f, by_both = P("fsdp"), P("fsdp", "ctx", None)
    in_specs = (by_both, by_f, P()) + (by_f,) * 10 + (P(), by_both)
    out_specs = (by_both, by_both) + (by_f,) * 10 + (P(),)
    return jax.shard_map(
        functools.partial(per_device, mesh.shape["fsdp"]),
        mesh=mesh,
        in_specs=in_specs,
        out_specs=out_specs,
        check_vma=False,
    )
```

```python
import functools
import math
from types import SimpleNamespace

import jax
import jax.numpy as jnp
from jax import lax
from jax.experimental import pallas as pl
from jax.experimental.pallas import tpu as pltpu
from jax.sharding import PartitionSpec as P

MESH = pl.DeviceIdType.MESH
F32 = jnp.float32
BF16 = jnp.bfloat16
norm_eps = 1e-05
masked_low = -1e30
CTX = 4
LANES = 128


def mm(left, right, left_dim=1, right_dim=0):
    return lax.dot_general(
        left, right, (((left_dim,), (right_dim,)), ((), ())), preferred_element_type=F32
    )


def norm_stats(rows):
    centre = jnp.mean(rows, axis=-1, keepdims=True)
    centred = rows - centre
    spread = jnp.mean(centred * centred, axis=-1, keepdims=True)
    scale = lax.rsqrt(spread + norm_eps)
    return centred * scale, scale


def norm_back(d_normed, gain_row, hat, scale):
    d_hat = d_normed * gain_row
    mean_d = jnp.mean(d_hat, axis=-1, keepdims=True)
    mean_dh = jnp.mean(d_hat * hat, axis=-1, keepdims=True)
    return scale * (d_hat - mean_d - hat * mean_dh)


class Sizes:
    def __init__(self, n_f, rows, width, ff, group, buckets, heads):
        self.n_f = n_f
        self.half = n_f // 2
        self.rows = rows
        self.width = width
        self.ff = ff
        self.group = group
        self.buckets = buckets
        self.heads = heads
        self.head = width // heads
        self.w_rows = width // n_f
        self.d_rows = ff // n_f
        self.own_ff = ff // CTX
        self.part = self.d_rows // CTX
        self.owned = n_f // CTX
        self.blocks = CTX * (CTX + 1) // 2


class Links:
    def __init__(self, send_sems, recv_sems):
        self.send_sems = send_sems
        self.recv_sems = recv_sems
        self.used = 0
        self.pending = []

    def copy(self, src, dst, index, arrival, device):
        return pltpu.make_async_remote_copy(
            src_ref=src,
            dst_ref=dst,
            send_sem=self.send_sems.at[index],
            recv_sem=self.recv_sems.at[arrival],
            device_id=device,
            device_id_type=MESH,
        )

    def send(self, src, dst, arrival, device):
        self.copy(src, dst, self.used, arrival, device).start()
        self.pending.append((src, self.used, device))
        self.used += 1

    def send_all(self, pairs, arrival, devices, size):
        for (src, dst), device in zip(pairs, devices):
            self.copy(src, dst, self.used, arrival, device).start()
        self.pending.append((size, self.used, devices[0]))
        self.used += 1

    def wait(self, dst, arrival, device):
        self.copy(dst, dst, 0, arrival, device).wait_recv()

    def drain(self):
        for src, index, device in self.pending:
            self.copy(src, src, index, 0, device).wait_send()
        self.pending = []


SENDS = 128


def layer_kernel(
    sizes,
    tok_in,
    seg_in,
    table_in,
    wqkv_in,
    wout_in,
    win_in,
    wdown_in,
    vec_in0,
    vec_in1,
    vec_in2,
    vec_in3,
    vec_in4,
    bias_in_in,
    rel_in,
    dy_in,
    out_ref,
    dx_ref,
    gqk_ref,
    gv_ref,
    gout_ref,
    gin_ref,
    gdown_ref,
    small_ref,
    *scratch_refs,
):
    s, sem = name_scratch(scratch_spec(sizes), scratch_refs[:-3])
    send_sems, recv_sems, own_sems = scratch_refs[-3:]
    n_f, half, rows = sizes.n_f, sizes.half, sizes.rows
    width, w_rows, d_rows, own_ff = sizes.width, sizes.w_rows, sizes.d_rows, sizes.own_ff
    part, out_part = sizes.part, sizes.w_rows // CTX
    head = sizes.head

    c = lax.axis_index("ctx")
    f = lax.axis_index("fsdp")
    side = c // 2
    core = c % 2
    place = f // 2
    par = f % 2
    sib = side * 2 + 1 - core
    opp = (1 - side) * 2 + core
    diag = (1 - side) * 2 + 1 - core

    def ctx_dev(index):
        return {"ctx": index, "fsdp": f}

    def f_dev(index):
        return {"ctx": c, "fsdp": index}

    partner = 2 * place + 1 - par

    def other_place(step):
        return lax.rem(place + step, half)

    links = Links(send_sems, recv_sems)

    barrier = pltpu.get_barrier_semaphore()
    for step in range(1, CTX):
        pl.semaphore_signal(
            barrier, inc=1, device_id=ctx_dev(lax.rem(c + step, CTX)), device_id_type=MESH
        )
    for step in range(1, n_f):
        pl.semaphore_signal(
            barrier, inc=1, device_id=f_dev(lax.rem(f + step, n_f)), device_id_type=MESH
        )

    own_copies, leaving = [], []

    def fetch(src, dst):
        made = pltpu.make_async_copy(src, dst, own_sems.at[len(own_copies)])
        own_copies.append(made)
        made.start()
        return made

    def keep(src, dst):
        made = pltpu.make_async_copy(src, dst, own_sems.at[len(own_copies)])
        own_copies.append(made)
        made.start()
        leaving.append(made)

    first_fetches = []
    for third in range(3):
        cols = pl.ds(pl.multiple_of(third * width + c * LANES, LANES), LANES)
        first_fetches.append(
            fetch(wqkv_in.at[:, cols], s.wq.at[f, :, third * LANES : (third + 1) * LANES])
        )
    first_fetches.append(fetch(tok_in, s.tok.at[c]))
    own_block = pl.ds(pl.multiple_of(c * LANES, LANES), LANES)
    later_fetches = [
        fetch(wdown_in.at[pl.ds(pl.multiple_of(c * part, 8), part), :], s.wd.at[f]),
        fetch(wout_in.at[:, own_block], s.wo.at[c, f]),
        fetch(dy_in, s.dy.at[c]),
    ]
    small_in = (vec_in0, vec_in1, vec_in2, vec_in3, vec_in4)
    small_fetches = [fetch(ref, s.ones[at]) for at, ref in enumerate(small_in)]
    small_fetches.append(fetch(bias_in_in, s.bias))
    table_fetches = [fetch(seg_in, s.seg), fetch(table_in, s.table), fetch(rel_in, s.rel)]
    hidden_fetch = fetch(win_in, s.win)
    for made in small_fetches:
        made.wait()
    for at in range(len(small_in)):
        s.vec[f, at : at + 1, 0:w_rows] = s.ones[at][...].astype(F32)
    for at in range(s.bias.shape[0]):
        size = s.bias.shape[1]
        s.vec[f, 5:6, at * size : (at + 1) * size] = s.bias[at : at + 1, :].astype(F32)
    hidden_fetch.wait()
    for at in range(CTX):

        @pl.when(c == at)
        def pick_hidden(at=at):
            starts = [index * d_rows + at * part for index in range(n_f)]
            s.wi[f] = jnp.concatenate([s.win[:, low : low + part] for low in starts], axis=1)

    for made in first_fetches + table_fetches:
        made.wait()

    pl.semaphore_wait(barrier, CTX - 1 + n_f - 1)

    peers = [f_dev(lax.rem(f + step, n_f)) for step in range(1, n_f)]
    far = [2 * other_place(step) + par for step in range(1, half)]
    others = [ctx_dev(lax.rem(c + step, CTX)) for step in range(1, CTX)]

    def to_peers(buf, first):
        piece = buf.at[f]
        links.send_all([(piece, piece)] * (n_f - 1), first, peers, buf.at[0 : n_f - 1])

    def from_peers(buf, first):
        links.wait(buf.at[0 : n_f - 1], first, peers[0])

    def to_group(buf, first):
        piece = buf.at[c]
        links.send_all([(piece, piece)] * (CTX - 1), first, others, buf.at[0 : CTX - 1])

    def from_group(buf, first):
        links.wait(buf.at[0 : CTX - 1], first, others[0])

    def spread(buf, first):
        piece = buf.at[f]
        links.send_all(
            [(piece, piece)] * (half - 1),
            first[0] + place,
            [f_dev(to) for to in far],
            buf.at[0 : half - 1],
        )
        links.send(piece, piece, first[1], f_dev(partner))

    def pass_on(buf, first):
        pairs = []
        for step in range(1, half):
            src = far[step - 1]
            links.wait(buf.at[src], first[0] + src // 2, f_dev(src))
            links.send(buf.at[src], buf.at[src], first[1], f_dev(partner))

    def settle(buf, first):
        links.wait(buf.at[0:half], first[1], f_dev(partner))

    for to in (sib, opp):
        links.send(s.tok.at[c], s.tok.at[c], sem.tok + c, ctx_dev(to))
    to_peers(s.vec, sem.vec)
    spread(s.wq, sem.wq)
    for made in later_fetches:
        made.wait()
    own_out = s.wo.at[c]

    ids = lax.broadcasted_iota(jnp.int32, (sizes.buckets, sizes.group), 0)
    onehot = (ids == s.table[...]).astype(BF16)
    s.hot[...] = onehot.astype(F32)
    s.bvec[...] = mm(s.rel[...], onehot)
    for h in range(2):
        row = s.bvec[pl.ds(2 * c + h, 1), :]
        for delta in range(CTX):
            now = row[:, delta * rows : (delta + 1) * rows]
            before = row[:, (delta - 1) * rows : delta * rows] if delta else now
            wide = jnp.broadcast_to(jnp.concatenate([now, before], axis=1), (rows, 2 * rows))
            turned = pltpu.roll(wide, 0, 1, stride=1, stride_axis=0)
            s.tile[h, delta] = turned[:, :rows]
    seg_f = s.seg[...].astype(F32)
    for at in range(CTX):
        piece = jnp.broadcast_to(seg_f[:, at * rows : (at + 1) * rows], (rows, rows))
        s.segk[at] = jnp.transpose(piece)
    key_pos = lax.broadcasted_iota(jnp.int32, (rows, rows), 0)
    query_pos = lax.broadcasted_iota(jnp.int32, (rows, rows), 1)
    for q_at in range(CTX):
        seg_q = jnp.broadcast_to(seg_f[:, q_at * rows : (q_at + 1) * rows], (rows, rows))
        for k_at in range(q_at + 1):
            seg_k = s.segk[k_at]
            allowed = (seg_k == 0.0) | (seg_k == seg_q)
            if q_at == k_at:
                allowed = allowed & (key_pos <= query_pos)
            for h in range(2):
                block = q_at * (q_at + 1) // 2 + k_at
                s.bm[h, block] = jnp.where(allowed, s.tile[h, q_at - k_at], masked_low)

    from_peers(s.vec, sem.vec)

    def joined(pieces, count, size):
        total = count * size
        spot = lax.broadcasted_iota(jnp.int32, (size, total), 1) % size
        which = lax.broadcasted_iota(jnp.int32, (size, total), 0)
        spreader = (spot == which).astype(BF16)
        flat = mm(pieces.astype(BF16), spreader)
        owner = lax.broadcasted_iota(jnp.int32, (count, total), 1) // size
        mine = owner == lax.broadcasted_iota(jnp.int32, (count, total), 0)
        return jnp.sum(jnp.where(mine, flat, 0.0), axis=0, keepdims=True)

    for at in range(5):
        s.vrow[at : at + 1, :] = joined(s.vec[:, at, 0:w_rows], n_f, w_rows)
    for at in range(CTX):

        @pl.when(c == at)
        def pick_bias(at=at):
            s.vrow[5:6, :] = joined(s.vec[:, 5, at * part : (at + 1) * part], n_f, part)

    gain_one, shift_one = s.vrow[0:1, :], s.vrow[1:2, :]
    gain_two, shift_two = s.vrow[2:3, :], s.vrow[3:4, :]
    bias_down_row, bias_in_row = s.vrow[4:5, :], s.vrow[5:6, :]

    step_rows = 64

    def row_loop(body, count=rows):
        def run(at, carried):
            body(pl.ds(pl.multiple_of(at * step_rows, step_rows), step_rows))
            return carried

        lax.fori_loop(0, count // step_rows, run, 0)

    def first_norm(chunk):
        def body(part):
            hat, scale = norm_stats(s.tok[chunk, part, :].astype(F32))
            s.fn[chunk, part, :] = (hat * gain_one + shift_one).astype(BF16)

        row_loop(body)

    def whole(buf, count, size, kept):
        if size % 16 == 0:
            return buf[...].reshape(count * size, buf.shape[2])
        for at in range(count):
            kept[at * size : (at + 1) * size, :] = buf[at]
        return kept[...]

    head_rows = lax.broadcasted_iota(jnp.int32, (LANES, rows), 0) // head

    def project(chunk):
        weights = whole(s.wq, n_f, w_rows, s.flat_wq)
        made = mm(s.fn[chunk], weights)
        queries = made[:, 0:LANES].astype(BF16).astype(F32) * (head ** -0.5)
        keys = made[:, LANES : 2 * LANES]
        values = made[:, 2 * LANES : 3 * LANES]
        s.k[chunk] = keys.astype(BF16)
        s.v[chunk] = values.astype(BF16)
        s.kt[chunk] = jnp.transpose(keys).astype(BF16)
        s.vt[chunk] = jnp.transpose(values).astype(BF16)
        turned = jnp.transpose(queries)
        for h in range(2):
            kept = jnp.where(head_rows == h, turned, 0.0)
            s.qt[h, chunk] = kept.astype(BF16)
            s.q[h, chunk] = jnp.transpose(kept).astype(BF16)

    first_norm(c)
    for to in (sib, opp):
        links.send(s.dy.at[c], s.dy.at[c], sem.dy + c, ctx_dev(to))
    pass_on(s.wq, sem.wq)
    to_peers(own_out, sem.wo[0])
    spread(s.wi, sem.wi)
    spread(s.wd, sem.wd)
    links.wait(s.tok.at[sib], sem.tok + sib, ctx_dev(sib))
    first_norm(sib)
    links.wait(s.tok.at[opp], sem.tok + opp, ctx_dev(opp))
    links.send(s.tok.at[opp], s.tok.at[opp], sem.tok + opp, ctx_dev(sib))
    first_norm(opp)


    def share_out(to, block):
        links.send(s.wo.at[block], s.wo.at[block], sem.wo[1] + block, ctx_dev(to))

    def wait_out(block, via):
        links.wait(s.wo.at[block], sem.wo[1] + block, ctx_dev(via))

    settle(s.wq, sem.wq)
    project(c)
    project(sib)
    project(opp)
    links.wait(s.tok.at[diag], sem.tok + diag, ctx_dev(sib))
    first_norm(diag)
    project(diag)
    from_peers(own_out, sem.wo[0])
    share_out(sib, c)
    share_out(opp, c)

    def attend_rows(chunk):
        first_block = chunk * (chunk + 1) // 2
        for h in range(2):
            top = jnp.full((1, rows), masked_low, F32)
            for k_at in range(chunk + 1):
                scores = mm(s.k[k_at], s.qt[h, chunk]) + s.bm[h, first_block + k_at]
                s.sc[h, k_at] = scores
                top = jnp.maximum(top, jnp.max(scores, axis=0, keepdims=True))
            lanes = slice(h * head, (h + 1) * head)
            total = jnp.zeros((1, rows), F32)
            mixed = jnp.zeros((head, rows), F32)
            for k_at in range(chunk + 1):
                weights = jnp.exp(s.sc[h, k_at] - top)
                total = total + jnp.sum(weights, axis=0, keepdims=True)
                rounded = weights.astype(BF16)
                s.e[h, first_block + k_at] = rounded
                mixed = mixed + mm(s.vt[k_at, lanes, :], rounded)
            inverse = 1.0 / total
            s.linv[chunk, h : h + 1, :] = inverse
            s.att_t[chunk, lanes, :] = mixed * inverse
        s.att[c, chunk] = jnp.transpose(s.att_t[chunk]).astype(BF16)

    def attend(turn):
        for which in range(2):
            pl.when(side == which)(functools.partial(attend_rows, (2 * which + turn) % CTX))

    def att_slot(owner, chunk):
        return owner * CTX + chunk

    def send_att(chunk):
        piece = s.att.at[c, chunk]
        for to in (sib, opp):
            links.send(piece, piece, sem.att + att_slot(c, chunk), ctx_dev(to))

    def wait_att(owner, chunk, via):
        links.wait(s.att.at[owner, chunk], sem.att + att_slot(owner, chunk), ctx_dev(via))

    def pass_att(chunk):
        wait_att(opp, chunk, opp)
        piece = s.att.at[opp, chunk]
        links.send(piece, piece, sem.att + att_slot(opp, chunk), ctx_dev(sib))

    mine = [lax.rem(2 * side + step, CTX) for step in range(CTX)]
    theirs = [lax.rem(2 * (1 - side) + step, CTX) for step in range(CTX)]
    attend(0)
    send_att(mine[0])
    attend(1)
    send_att(mine[1])
    pass_on(s.wi, sem.wi)
    pass_att(theirs[0])
    wait_out(opp, opp)
    share_out(sib, opp)
    attend(2)
    send_att(mine[2])
    pass_on(s.wd, sem.wd)
    pass_att(theirs[1])
    links.wait(s.dy.at[opp], sem.dy + opp, ctx_dev(opp))
    links.send(s.dy.at[opp], s.dy.at[opp], sem.dy + opp, ctx_dev(sib))
    attend(3)
    send_att(mine[3])

    wait_out(sib, sib)
    wait_out(diag, sib)
    for block in range(CTX):
        cols = slice(block * LANES, (block + 1) * LANES)
        if w_rows % 16 == 0:
            s.wo_flat[:, cols] = s.wo[block].reshape(width, LANES)
        else:
            for at in range(n_f):
                s.wo_flat[at * w_rows : (at + 1) * w_rows, cols] = s.wo[block, at]

    def gather_att(chunk):
        wait_att(sib, chunk, sib)
        wait_att(diag, chunk, sib)

    def feed(chunk):
        gather_att(chunk)
        mixed = jnp.zeros((rows, width), F32)
        for owner in range(CTX):
            mixed += mm(
                s.att[owner, chunk], s.wo_flat[owner * LANES : (owner + 1) * LANES, :]
            )
        s.mid[...] = mixed + s.tok[chunk].astype(F32)

        def normed(rng):
            hat, scale = norm_stats(s.mid[rng, :])
            s.sn[chunk, rng, :] = (hat * gain_two + shift_two).astype(BF16)

        row_loop(normed)
        s.inner[chunk] = mm(s.sn[chunk], whole(s.wi, n_f, w_rows, s.flat_wi))

    def feed_back(chunk):
        w_down = whole(s.wd, n_f, part, s.flat_wd)
        s.dact[...] = mm(s.dy[chunk], w_down, 1, 1)

        def gelu(rng):
            inner = s.inner[chunk, rng, :] + bias_in_row
            phi = 0.5 + 0.5 * lax.erf(inner * (2.0 ** -0.5))
            slope = phi + inner * (jnp.exp(-0.5 * inner * inner) * (1.0 / math.sqrt(2.0 * math.pi)))
            s.actv[chunk, rng, :] = (inner * phi).astype(BF16)
            s.din[chunk, rng, :] = (s.dact[rng, :] * slope).astype(BF16)

        row_loop(gelu)
        return mm(s.din[chunk], whole(s.wi, n_f, w_rows, s.flat_wi), 1, 1)

    def scatter_first(group, first, part):
        group[0][...] = part.astype(BF16)
        links.send(group[0], group[1], first[0], ctx_dev(sib))

    def scatter_second(group, first, part):
        links.wait(group[1], first[0], ctx_dev(sib))
        group[2][...] = (part + group[1][...].astype(F32)).astype(BF16)
        links.send(group[2], group[3], first[1], ctx_dev(opp))

    def scatter_third(group, first, part):
        group[4][...] = part.astype(BF16)
        links.send(group[4], group[5], first[2], ctx_dev(sib))

    def scatter_wait(group, first):
        links.wait(group[5], first[2], ctx_dev(sib))
        links.wait(group[3], first[1], ctx_dev(opp))

    def scatter_sum(group, part):
        return group[3][part, :].astype(F32) + group[5][part, :].astype(F32)

    settle(s.wi, sem.wi)
    feed(diag)
    pass_att(theirs[2])
    feed(opp)
    pass_att(theirs[3])
    settle(s.wd, sem.wd)
    links.wait(s.dy.at[diag], sem.dy + diag, ctx_dev(sib))
    scatter_first(s.rs_s, sem.rs_s, feed_back(diag))
    scatter_second(s.rs_s, sem.rs_s, feed_back(opp))
    feed(sib)
    links.wait(s.dy.at[sib], sem.dy + sib, ctx_dev(sib))
    scatter_third(s.rs_s, sem.rs_s, feed_back(sib))
    feed(c)
    s.dsec[...] = feed_back(c)

    def even_pieces(group, left, right, cols, size):
        for at in range(left.shape[2] // LANES):
            lhs = left[:, :, at * LANES : (at + 1) * LANES].reshape(CTX * rows, LANES)
            made = mm(lhs, right[...].reshape(CTX * rows, cols), 0, 0).astype(BF16)
            for piece in range(LANES // size):
                to = at * (LANES // size) + piece
                group[0][to % 2, to // 2] = made[piece * size : (piece + 1) * size, :]

    def grad_pair(group, first):
        for to in far:
            links.send(
                group[0].at[1 - par, to // 2], group[1].at[to // 2], first[0] + to // 2, f_dev(partner)
            )
        links.send(group[0].at[1 - par, place], group[1].at[place], first[0] + place, f_dev(partner))

    def grad_step(group, first, step):
        at = far[step] // 2 if step < half - 1 else place
        links.wait(group[1].at[at], first[0] + at, f_dev(partner))
        group[2][at] = (group[0][par, at].astype(F32) + group[1][at].astype(F32)).astype(BF16)
        if step < half - 1:
            links.send(group[2].at[at], group[3].at[place], first[1], f_dev(far[step]))

    def grad_steps(group, first, low=0, high=half):
        for step in range(low, high):
            grad_step(group, first, step)

    def grad_even_third(group, first):
        links.wait(group[3].at[0 : half - 1], first[1], f_dev(far[0]))
        total = group[2][place].astype(F32)
        for src in far:
            total += group[3][src // 2].astype(F32)
        group[4][c] = total.astype(BF16)
        to_group(group[4], first[2])

    def grad_direct(group, first):
        pairs = [
            (group[0].at[lax.rem(f + step, n_f)], group[1].at[f]) for step in range(1, n_f)
        ]
        links.send_all(pairs, first[0], peers, group[1].at[0 : n_f - 1])

    def grad_direct_sum(group, first):
        from_peers(group[1], first[0])
        total = group[0][f].astype(F32)
        for step in range(1, n_f):
            total += group[1][lax.rem(f + step, n_f)].astype(F32)
        group[2][c] = total.astype(BF16)
        to_group(group[2], first[1])

    even_pieces(s.gd, s.actv, s.dy, width, part)
    grad_pair(s.gd, sem.gd)
    even_pieces(s.gi, s.sn, s.din, own_ff, w_rows)
    grad_pair(s.gi, sem.gi)
    w_down = whole(s.wd, n_f, part, s.flat_wd)
    scatter_first(s.rs_o, sem.rs_o, mm(s.actv[diag], w_down))
    scatter_third(s.rs_o, sem.rs_o, mm(s.actv[sib], w_down))
    grad_steps(s.gd, sem.gd, 0, half // 2)

    scatter_wait(s.rs_s, sem.rs_s)
    s.vg[...] = jnp.zeros_like(s.vg)

    def second_back(rng):
        hat, scale = norm_stats(s.mid[rng, :])
        d_second = s.dsec[rng, :] + scatter_sum(s.rs_s, rng)
        d_result = s.dy[c, rng, :].astype(F32)
        d_middle = d_result + norm_back(d_second, gain_two, hat, scale)
        s.dmid[rng, :] = d_middle
        s.dmx[rng, :] = d_middle.astype(BF16)
        s.vg[2:3, :] += jnp.sum(d_second * hat, axis=0, keepdims=True)
        s.vg[3:4, :] += jnp.sum(d_second, axis=0, keepdims=True)
        s.vg[4:5, :] += jnp.sum(d_result, axis=0, keepdims=True)

    row_loop(second_back)
    d_att = mm(s.wo_flat[...], s.dmx[...], 1, 1)
    s.dat_out[...] = d_att.astype(BF16).reshape(CTX, LANES, rows)
    for to in (opp, diag, sib):
        links.send(s.dat_out.at[to], s.dat.at[c], sem.dat + c, ctx_dev(to))
    s.dat[c] = s.dat_out[c]
    for owner in range(CTX):
        made = mm(s.att[owner, c], s.dmx[...], 0, 0).astype(BF16)
        for piece in range(LANES // w_rows):
            at = owner * (LANES // w_rows) + piece
            for part_at in range(CTX):
                low = piece * w_rows + part_at * out_part
                s.go_own[part_at % 2, part_at // 2, at] = made[low : low + out_part, :]
    links.send(s.go_own.at[1 - core], s.go_core, sem.go_core, ctx_dev(sib))
    grad_steps(s.gd, sem.gd, half // 2, half)
    links.wait(s.go_core, sem.go_core, ctx_dev(sib))
    s.go_two[...] = (
        s.go_own[core].astype(F32) + s.go_core[...].astype(F32)
    ).astype(BF16)
    links.send(s.go_two.at[1 - side], s.go_side, sem.go_side, ctx_dev(opp))
    scatter_second(s.rs_o, sem.rs_o, mm(s.actv[opp], w_down))
    s.outp[...] = s.mid[...] + mm(s.actv[c], w_down) + bias_down_row
    for at in range(CTX):

        def bias_rows(rng, at=at):
            s.vg[5:6, :] += jnp.sum(s.din[at, rng, :].astype(F32), axis=0, keepdims=True)

        row_loop(bias_rows)
    grad_steps(s.gi, sem.gi, 0, half // 2)

    for src in (sib, opp, diag):
        links.wait(s.dat.at[src], sem.dat + src, ctx_dev(src))
    for at in range(CTX):
        got = s.dat[at].astype(F32)
        for h in range(2):
            part = slice(h * head, (h + 1) * head)
            scaled = (got * s.linv[at, h : h + 1, :]).astype(BF16)
            kept = jnp.where(head_rows == h, scaled.astype(F32), 0.0)
            s.dat_t[h, at] = kept.astype(BF16)
            s.dat_n[h, at] = jnp.transpose(kept).astype(BF16)
            s.delta[at, h : h + 1, :] = jnp.sum(
                kept[part, :] * s.att_t[at, part, :], axis=0, keepdims=True
            )
        s.dqt[at] = jnp.zeros((LANES, rows), F32)
        s.dk[at] = jnp.zeros((rows, LANES), F32)
    s.dbm[...] = jnp.zeros_like(s.dbm)

    def block_pair(q_at, k_at):
        block = q_at * (q_at + 1) // 2 + k_at
        values = s.v[k_at]
        for h in range(2):
            lanes = slice(h * head, (h + 1) * head)
            d_probs = mm(values, s.dat_t[h, q_at])
            rounded = s.e[h, block]
            d_scores = rounded.astype(F32) * (d_probs - s.delta[q_at, h : h + 1, :])
            s.dbm[h, q_at - k_at] += d_scores
            low = d_scores.astype(BF16)
            s.dk[k_at] += mm(low, s.q[h, q_at])
            s.dqt[q_at, lanes, :] += mm(s.kt[k_at, lanes, :], low)

    def query_row(upper):
        def run(lower, carried):
            shift = side * (CTX - 1 - upper - lower)
            block_pair(upper + shift, lower + shift)
            return carried

        lax.fori_loop(0, upper + 1, run, 0)

    def pack(chunk):
        s.dp[chunk, :, 0:LANES] = (jnp.transpose(s.dqt[chunk]) * (head ** -0.5)).astype(BF16)
        s.dp[chunk, :, LANES : 2 * LANES] = s.dk[chunk].astype(BF16)

    w_qkv = whole(s.wq, n_f, w_rows, s.flat_wq)

    def back_first(chunk):
        s.dsec[...] = mm(s.dp[chunk], w_qkv, 1, 1)

        def add_rows(rng):
            part_rows = s.dsec[rng, :]
            s.vg[0:1, :] += jnp.sum(s.fn[chunk, rng, :].astype(F32) * part_rows, axis=0, keepdims=True)
            s.vg[1:2, :] += jnp.sum(part_rows, axis=0, keepdims=True)

        return add_rows

    def value_grads(k_at):
        made = jnp.zeros((rows, LANES), F32)
        for q_at in range(k_at, CTX):
            block = q_at * (q_at + 1) // 2 + k_at
            for h in range(2):
                made += mm(s.e[h, block], s.dat_n[h, q_at])
        s.dp[k_at, :, 2 * LANES : 3 * LANES] = made.astype(BF16)

    def qkv_pieces(group, cols):
        for at in range(width // LANES):
            lhs = s.fn[:, :, at * LANES : (at + 1) * LANES].reshape(CTX * rows, LANES)
            rhs = s.dp[:, :, cols].reshape(CTX * rows, cols.stop - cols.start)
            made = mm(lhs, rhs, 0, 0).astype(BF16)
            for piece in range(LANES // w_rows):
                to = at * (LANES // w_rows) + piece
                got = made[piece * w_rows : (piece + 1) * w_rows, :]
                if len(group) == 5:
                    group[0][to % 2, to // 2] = got
                else:
                    group[0][to] = got

    for at in range(CTX):
        value_grads(at)
    qkv_pieces(s.gv, slice(2 * LANES, 3 * LANES))
    grad_pair(s.gv, sem.gv)
    query_row(3)
    grad_steps(s.gi, sem.gi, half // 2, half)
    links.wait(s.go_side, sem.go_side, ctx_dev(opp))
    for at in range(n_f):
        s.go[0][at % 2, at // 2] = (
            s.go_two[side, at].astype(F32) + s.go_side[at].astype(F32)
        ).astype(BF16)
    grad_pair(s.go, sem.go)
    query_row(2)
    pack(diag)
    pack(opp)
    sums = back_first(diag)
    scatter_first(s.rs_f, sem.rs_f, s.dsec[...])
    row_loop(sums)
    sums = back_first(opp)
    scatter_second(s.rs_f, sem.rs_f, s.dsec[...])
    row_loop(sums)
    grad_steps(s.gv, sem.gv)
    query_row(1)
    grad_even_third(s.gd, sem.gd)
    grad_steps(s.go, sem.go)
    query_row(0)
    pack(sib)
    pack(c)
    qkv_pieces(s.gq, slice(0, 2 * LANES))
    grad_direct(s.gq, sem.gq)
    grad_even_third(s.gv, sem.gv)
    sums = back_first(sib)
    scatter_third(s.rs_f, sem.rs_f, s.dsec[...])
    row_loop(sums)
    sums = back_first(c)
    row_loop(sums)

    for h in range(2):
        pieces = []
        for delta in range(CTX):
            block = s.dbm[h, delta]
            wide = jnp.concatenate([block, jnp.zeros((rows, rows), F32)], axis=1)
            count = rows
            while count > 1:
                count //= 2
                turned = pltpu.roll(wide[count : 2 * count, :], 2 * rows - count, 1)
                wide = wide[0:count, :] + turned
            pieces.append(wide)
        total = []
        for delta in range(CTX):
            here = pieces[delta][:, 0:rows]
            if delta + 1 < CTX:
                here = here + pieces[delta + 1][:, rows : 2 * rows]
            total.append(here)
        dist = jnp.concatenate(total, axis=1)
        bucket_sums = lax.dot_general(
            jnp.broadcast_to(dist, (8, sizes.group)),
            s.hot[...],
            (((1,), (1,)), ((), ())),
            preferred_element_type=F32,
            precision=lax.Precision.HIGHEST,
        )
        s.vg[6 + h : 7 + h, 0 : sizes.buckets] = bucket_sums[0:1, :]

    s.vg[0:1, :] = (s.vg[0:1, :] - shift_one * s.vg[1:2, :]) / gain_one
    for to in range(n_f):
        s.vgp[to, :, 0:w_rows] = s.vg[:, to * w_rows : (to + 1) * w_rows]
        s.vgp[to, 6:8, 0 : sizes.buckets] = s.vg[6:8, 0 : sizes.buckets]
    pairs = [(s.vgp.at[lax.rem(f + step, n_f)], s.vgf.at[f]) for step in range(1, n_f)]
    links.send_all(pairs, sem.vgf, peers, s.vgf.at[0 : n_f - 1])

    scatter_wait(s.rs_f, sem.rs_f)

    def first_back(rng):
        hat, scale = norm_stats(s.tok[c, rng, :].astype(F32))
        d_first = s.dsec[rng, :] + scatter_sum(s.rs_f, rng)
        d_x = s.dmid[rng, :] + norm_back(d_first, gain_one, hat, scale)
        s.dx[rng, :] = d_x.astype(BF16)

    row_loop(first_back)
    keep(s.dx, dx_ref)
    grad_even_third(s.gi, sem.gi)
    grad_direct_sum(s.gq, sem.gq)
    from_peers(s.vgf, sem.vgf)
    total = s.vgp[f]
    for step in range(1, n_f):
        total += s.vgf[lax.rem(f + step, n_f)]
    s.vgc[c] = total
    to_group(s.vgc, sem.vgc)
    grad_even_third(s.go, sem.go)

    scatter_wait(s.rs_o, sem.rs_o)
    s.out[...] = (
        s.outp[...] + s.rs_o[3][...].astype(F32) + s.rs_o[5][...].astype(F32)
    ).astype(BF16)
    keep(s.out, out_ref)
    from_group(s.gd[4], sem.gd[2])
    keep(s.gd[4], gdown_ref)
    from_group(s.gv[4], sem.gv[2])
    keep(s.gv[4], gv_ref)
    from_group(s.gq[2], sem.gq[1])
    keep(s.gq[2], gqk_ref)
    from_group(s.vgc, sem.vgc)
    keep(s.vgc, small_ref)
    from_group(s.go[4], sem.go[2])
    keep(s.go[4], gout_ref)
    from_group(s.gi[4], sem.gi[2])
    keep(s.gi[4], gin_ref)
    links.drain()
    for made in leaving:
        made.wait()


def finish_kernel(
    sizes,
    out_in,
    dx_in,
    gqk_in,
    gv_in,
    gout_in,
    gin_in,
    gdown_in,
    small_in,
    out_ref,
    dx_ref,
    gqkv_ref,
    gout_ref,
    gin_ref,
    gdown_ref,
    gg1_ref,
    gs1_ref,
    gg2_ref,
    gs2_ref,
    gbi_ref,
    gbd_ref,
    grel_ref,
    gqkv,
    gout,
    gin,
    gdown,
    gqk_low,
    gv_low,
    gout_low,
    gin_low,
    gdown_low,
    out_low,
    dx_low,
    small,
    gg1,
    gs1,
    gg2,
    gs2,
    gbi,
    gbd,
    grel,
    sems,
):
    made = []

    def start(src, dst):
        copy = pltpu.make_async_copy(src, dst, sems.at[len(made)])
        copy.start()
        made.append(copy)
        return copy

    loads = [
        start(gdown_in, gdown_low),
        start(gin_in, gin_low),
        start(gqk_in, gqk_low),
        start(gout_in, gout_low),
    ]
    loads += [start(out_in, out_low), start(dx_in, dx_low), start(gv_in, gv_low)]
    loads.append(start(small_in, small))
    width, own_ff = sizes.width, sizes.own_ff
    stores = []
    loads[4].wait()
    stores.append(start(out_low, out_ref))
    loads[5].wait()
    stores.append(start(dx_low, dx_ref))
    loads[0].wait()
    part = sizes.part
    for at in range(CTX):
        lines = slice(at * part, (at + 1) * part)
        gdown[lines, :] = gdown_low[at].astype(F32)
        stores.append(start(gdown.at[lines, :], gdown_ref.at[lines, :]))
    loads[1].wait()
    for index in range(sizes.n_f):
        lanes = slice(index * part, (index + 1) * part)
        joined = jnp.concatenate([gin_low[at, :, lanes].astype(F32) for at in range(CTX)], axis=1)
        gin[:, index * CTX * part : (index + 1) * CTX * part] = joined
    stores.append(start(gin, gin_ref))
    loads[2].wait()
    loads[6].wait()
    for at in range(CTX):
        for third in range(3):
            low = third * width + at * LANES
            if third == 2:
                got = gv_low[at]
            else:
                got = gqk_low[at, :, third * LANES : (third + 1) * LANES]
            gqkv[:, low : low + LANES] = got.astype(F32)
    stores.append(start(gqkv, gqkv_ref))
    loads[3].wait()
    out_part = sizes.w_rows // CTX
    for at in range(CTX):
        gout[at * out_part : (at + 1) * out_part, :] = gout_low[at].astype(F32)
    stores.append(start(gout, gout_ref))
    loads[7].wait()
    total = jnp.sum(small[...], axis=0)
    for at, ref in enumerate((gg1, gs1, gg2, gs2, gbd)):
        ref[...] = total[at : at + 1, 0 : sizes.w_rows]
    size = gbi.shape[1]
    hidden = jnp.concatenate([small[at, 5:6, 0:part] for at in range(CTX)], axis=1)
    for at in range(gbi.shape[0]):
        gbi[at : at + 1, :] = hidden[:, at * size : (at + 1) * size]
    for at in range(CTX):
        grel[2 * at : 2 * at + 2, :] = small[at, 6:8, 0 : sizes.buckets]
    small_pairs = (
        (gg1, gg1_ref),
        (gs1, gs1_ref),
        (gg2, gg2_ref),
        (gs2, gs2_ref),
        (gbi, gbi_ref),
        (gbd, gbd_ref),
        (grel, grel_ref),
    )
    for src, dst in small_pairs:
        stores.append(start(src, dst))
    for copy in stores:
        copy.wait()


def scratch_spec(z):
    rows, width, group = z.rows, z.width, z.group
    blocks = CTX * (CTX + 1) // 2
    act = (CTX, rows, width)
    hidden = (CTX, rows, z.own_ff)
    tall = (CTX, rows, LANES)
    wide = (CTX, LANES, rows)
    squares = (2, CTX, rows, rows)

    def scatter():
        flat = ((rows, width), BF16)
        landing = ((rows, width), BF16, 1)
        return [flat, landing, flat, landing, flat, landing]

    def even(size, cols):
        part = (z.half, size, cols)
        return [
            ((2,) + part, BF16),
            (part, BF16, z.half),
            (part, BF16),
            (part, BF16, 1),
            ((CTX, size, cols), BF16, 1),
        ]

    def direct(size, cols):
        whole = (z.n_f, size, cols)
        return [(whole, BF16), (whole, BF16, 1), ((CTX, size, cols), BF16, 1)]

    out_part = z.w_rows // CTX
    out_rows = (z.n_f, out_part, width)
    spec = dict(
        tok=(act, BF16, CTX),
        dy=(act, BF16, CTX),
        fn=(act, BF16),
        wq=((z.n_f, z.w_rows, 3 * LANES), BF16, z.half, 1),
        wo=((CTX, z.n_f, z.w_rows, LANES), BF16, 1, CTX),
        wo_flat=((width, width), BF16),
        wi=((z.n_f, z.w_rows, z.own_ff), BF16, z.half, 1),
        wd=((z.n_f, z.part, width), BF16, z.half, 1),
        vec=((z.n_f, 8, max(z.d_rows, LANES)), F32, 1),
        ones=[((1, z.w_rows), BF16)] * 5,
        bias=((max(1, z.d_rows // LANES), min(LANES, z.d_rows)), BF16),
        seg=((1, group), jnp.int32),
        table=((1, group), jnp.int32),
        rel=((z.heads, z.buckets), BF16),
        win=((z.w_rows, z.ff), BF16),
        out=((rows, width), BF16),
        dx=((rows, width), BF16),
        vrow=((8, width), F32),
        hot=((z.buckets, group), F32),
        bvec=((8, group), F32),
        tile=(squares, F32),
        segk=((CTX, rows, rows), F32),
        bm=((2, blocks, rows, rows), F32),
        k=(tall, BF16),
        v=(tall, BF16),
        kt=(wide, BF16),
        vt=(wide, BF16),
        qt=((2,) + wide, BF16),
        q=((2,) + tall, BF16),
        sc=(squares, F32),
        e=((2, blocks, rows, rows), BF16),
        acc=((LANES, rows), F32),
        linv=((CTX, 8, rows), F32),
        att_t=(wide, F32),
        att=((CTX,) + tall, BF16, CTX * CTX),
        mid=((rows, width), F32),
        sn=(act, BF16),
        inner=((CTX, rows, z.own_ff), F32),
        dact=((rows, z.own_ff), F32),
        actv=(hidden, BF16),
        din=(hidden, BF16),
        dsec=((rows, width), F32),
        outp=((rows, width), F32),
        dmid=((rows, width), F32),
        dmx=((rows, width), BF16),
        dat_out=(wide, BF16),
        dat=(wide, BF16, CTX),
        dat_t=((2,) + wide, BF16),
        dat_n=((2,) + tall, BF16),
        delta=((CTX, 8, rows), F32),
        dqt=(wide, F32),
        dbm=(squares, F32),
        dk=(tall, F32),
        dp=((CTX, rows, 3 * LANES), BF16),
        vg=((8, width), F32),
        vgp=((z.n_f, 8, LANES), F32),
        vgf=((z.n_f, 8, LANES), F32, 1),
        vgc=((CTX, 8, LANES), F32, 1),
        rs_s=scatter(),
        rs_o=scatter(),
        rs_f=scatter(),
        gq=direct(z.w_rows, 2 * LANES),
        gv=even(z.w_rows, LANES),
        gi=even(z.w_rows, z.own_ff),
        gd=even(z.part, width),
        go=even(out_part, width),
        go_own=((2, 2) + out_rows, BF16),
        go_core=((2,) + out_rows, BF16, 1),
        go_two=((2,) + out_rows, BF16),
        go_side=(out_rows, BF16, 1),
    )
    if z.w_rows % 16:
        spec.update(
            flat_wq=((width, 3 * LANES), BF16),
            flat_wi=((width, z.own_ff), BF16),
        )
    else:
        spec.update(flat_wq=((8, LANES), BF16), flat_wi=((8, LANES), BF16))
    flat_shape = (z.own_ff, width) if z.part % 16 else (8, LANES)
    spec.update(flat_wd=(flat_shape, BF16))
    return spec


def scratch_items(spec):
    for item in spec.values():
        if isinstance(item, list):
            yield from item
        else:
            yield item


def name_scratch(spec, refs):
    refs = iter(refs)
    by_name, first, used = {}, {}, 0
    for name, item in spec.items():
        entries = item if isinstance(item, list) else [item]
        held, starts = [], []
        for entry in entries:
            held.append(next(refs))
            for count in entry[2:]:
                starts.append(used)
                used += count
        by_name[name] = held if isinstance(item, list) else held[0]
        if starts:
            first[name] = starts if isinstance(item, list) or len(starts) > 1 else starts[0]
    return SimpleNamespace(**by_name), SimpleNamespace(**first)


def per_device(
    n_f,
    tokens,
    segment_ids,
    bucket_table,
    w_qkv,
    w_out,
    w_in,
    w_down,
    gain_one,
    shift_one,
    gain_two,
    shift_two,
    bias_in,
    bias_down,
    rel_bias,
    cotangent,
):
    sizes = Sizes(
        n_f,
        tokens.shape[1],
        tokens.shape[2],
        w_in.shape[1],
        segment_ids.shape[1],
        rel_bias.shape[0],
        rel_bias.shape[1],
    )
    rows, width, w_rows, d_rows = sizes.rows, sizes.width, sizes.w_rows, sizes.d_rows
    vmem = pl.BlockSpec(memory_space=pltpu.VMEM)
    far = pl.BlockSpec(memory_space=pltpu.HBM)
    spec = scratch_spec(sizes)
    n_recv = sum(sum(item[2:]) for item in scratch_items(spec))
    bias_shape = (max(1, d_rows // LANES), min(LANES, d_rows))
    shaped = jax.ShapeDtypeStruct
    made = pl.pallas_call(
        functools.partial(layer_kernel, sizes),
        out_shape=[
            shaped((rows, width), BF16),
            shaped((rows, width), BF16),
            shaped((CTX, w_rows, 2 * LANES), BF16),
            shaped((CTX, w_rows, LANES), BF16),
            shaped((CTX, w_rows // CTX, width), BF16),
            shaped((CTX, w_rows, sizes.own_ff), BF16),
            shaped((CTX, sizes.part, width), BF16),
            shaped((CTX, 8, LANES), F32),
        ],
        in_specs=[far] * 15,
        out_specs=[far] * 8,
        scratch_shapes=[pltpu.VMEM(item[0], item[1]) for item in scratch_items(spec)]
        + [
            pltpu.SemaphoreType.DMA((SENDS if n_f == 8 else 8 * n_f,)),
            pltpu.SemaphoreType.DMA((n_recv,)),
            pltpu.SemaphoreType.DMA((26,)),
        ],
        compiler_params=pltpu.CompilerParams(
            collective_id=0, has_side_effects=True, vmem_limit_bytes=60 * 1024 * 1024
        ),
        name="layer",
    )(
        tokens[0],
        segment_ids,
        bucket_table[None],
        w_qkv,
        w_out,
        w_in,
        w_down,
        gain_one[None],
        shift_one[None],
        gain_two[None],
        shift_two[None],
        bias_down[None],
        bias_in.reshape(bias_shape),
        jnp.transpose(rel_bias),
        cotangent[0],
    )
    outs = [
        ((rows, width), BF16),
        ((rows, width), BF16),
        ((w_rows, 3 * width), F32),
        ((w_rows, width), F32),
        ((w_rows, sizes.ff), F32),
        ((d_rows, width), F32),
        ((1, w_rows), F32),
        ((1, w_rows), F32),
        ((1, w_rows), F32),
        ((1, w_rows), F32),
        (bias_shape, F32),
        ((1, w_rows), F32),
        ((sizes.heads, sizes.buckets), F32),
    ]
    done = pl.pallas_call(
        functools.partial(finish_kernel, sizes),
        out_shape=[shaped(shape, kind) for shape, kind in outs],
        in_specs=[far] * 8,
        out_specs=[far] * 13,
        scratch_shapes=[pltpu.VMEM(shape, kind) for shape, kind in outs[2:6]]
        + [pltpu.VMEM(item.shape, item.dtype) for item in made[2:7] + made[0:2] + made[7:8]]
        + [pltpu.VMEM(shape, kind) for shape, kind in outs[6:]]
        + [pltpu.SemaphoreType.DMA((28,))],
        compiler_params=pltpu.CompilerParams(vmem_limit_bytes=60 * 1024 * 1024),
        name="finish",
    )(*made)
    return (
        done[0][None],
        done[1][None],
        done[2],
        done[3],
        done[4],
        done[5],
        done[6][0],
        done[7][0],
        done[8][0],
        done[9][0],
        done[10].reshape(-1),
        done[11][0],
        jnp.transpose(done[12]),
    )


def solution(mesh):
    by_f, by_both = P("fsdp"), P("fsdp", "ctx", None)
    in_specs = (by_both, by_f, P()) + (by_f,) * 10 + (P(), by_both)
    out_specs = (by_both, by_both) + (by_f,) * 10 + (P(),)
    return jax.shard_map(
        functools.partial(per_device, mesh.shape["fsdp"]),
        mesh=mesh,
        in_specs=in_specs,
        out_specs=out_specs,
        check_vma=False,
    )
```
